128 devices in a mesh: row: 16 (over z, y_hi, core), col: 4 (over x), dp: 2 (over y_lo).
Axes of the slice: x: 4, y: 4 (y_hi: 2, y_lo: 2; y = y_hi * 2 + y_lo), z: 4, core: 2. Of those that a mesh axis runs over, the one named last changes fastest.
Arguments:
- activations: bfloat16 [2, 1536, 4096], P('dp', 'row', 'col'), may hold values from -6 to 6
- cotangent: bfloat16 [2, 1536, 4096], P('dp', 'row', 'col'), may hold values from -6 to 6
- gate_weight: bfloat16 [4096, 8192], P('col', 'row'), may hold values from -0.09375 to 0.09375
- up_weight: bfloat16 [4096, 8192], P('col', 'row'), may hold values from -0.09375 to 0.09375
- down_weight: bfloat16 [8192, 4096], P('row', 'col'), may hold values from -0.0625 to 0.0625
- probes: bfloat16 [2, 4096, 8192], P(None, 'col', 'row'), may hold values from -1 to 1, as said below
Outputs:
- outputs: bfloat16 [2, 1536, 4096], P('dp', 'row', 'col')
- diag_estimate: float32 [4096, 8192], P('col', ('row', 'dp'))
The draws below stay inside these ranges and needn't reach their ends.
Inputs may be any that keep to these rules, and one draw needn't show every extreme that they name: `probes`: every entry is +1 or -1.
All inputs are finite; a program needn't handle non-finite values.
Results may differ from the reference program's by a relative error of at most 0.005.
Values may be sent and summed in bfloat16 or wider, within the bound.
No kernel may reach another device: no remote copies, remote signals or barrier semaphores. Data moves between devices by JAX's collectives and lax.ppermute only.
A program may use at most 128 MiB of HBM per device.

```python
import jax
import jax.numpy as jnp

D = 4096
F = 8192
TOK = 1536
NPROBE = 2
GROUPS = 2


def draw_probes(key, part):
    flips = jax.random.bernoulli(key, 0.5, (NPROBE, D, F))
    return jnp.where(flips, 1.0, -1.0).astype(jnp.float32).astype(jnp.bfloat16)


def levels(rng, dims, shards, low, largest):
    level, own = 1.0, jax.random.fold_in(rng, 6)
    for dim, blocks in shards:
        draws = jnp.exp(jax.random.uniform(jax.random.fold_in(own, dim), (blocks,), jnp.float32, low / len(shards), largest / len(shards)))
        level = level * jnp.repeat(draws, dims[dim] // blocks).reshape([-1 if axis == dim else 1 for axis in range(len(dims))])
    return level


def normal_values(key, shape, deviation, most, cuts=(), held_as=jnp.bfloat16):
    array = jax.random.normal(key, shape, jnp.float32) * deviation
    if len(cuts) > 0:
        array = levels(key, shape, cuts, -0.22, 0.18) * array
    return jnp.clip(array, min=-most, max=most).astype(held_as)


def setup_inputs(seed: int = 0) -> dict:
    splits = jax.random.split(jax.random.key(seed), 7)
    return {
        "activations": normal_values(splits[0], (GROUPS, TOK, D), 1.0, 6.0, ((0, 2), (1, 16), (2, 4))),
        "cotangent": normal_values(splits[1], (GROUPS, TOK, D), 1.0, 6.0, ((0, 2), (1, 16), (2, 4))),
        "gate_weight": normal_values(splits[2], (D, F), D ** -0.5, 0.09375, ((0, 4), (1, 16))),
        "up_weight": normal_values(splits[3], (D, F), D ** -0.5, 0.09375, ((0, 4), (1, 16))),
        "down_weight": normal_values(splits[4], (F, D), F ** -0.5, 0.0625, ((0, 16), (1, 4))),
        "probes": draw_probes(jax.random.fold_in(splits[6], 71), 0),
    }


def curvature_terms(features, cot_rows, gate_weight, up_weight, down_weight):
    gate_sum = jnp.dot(features, gate_weight, preferred_element_type=jnp.float32)
    up_sum = jnp.dot(features, up_weight, preferred_element_type=jnp.float32)
    error_sum = jnp.dot(cot_rows, down_weight.T, preferred_element_type=jnp.float32)
    sigma = jax.nn.sigmoid(gate_sum)
    hidden = (gate_sum * sigma * up_sum).astype(jnp.bfloat16)
    bending = error_sum * up_sum * sigma * (1.0 - sigma) * (2.0 + gate_sum * (1.0 - 2.0 * sigma))
    return hidden, bending


def reference(activations, cotangent, gate_weight, up_weight, down_weight, probes):
    results = []
    total = jnp.zeros((D, F), jnp.float32)
    for group in range(GROUPS):
        features = activations[group]
        hidden, bending = curvature_terms(features, cotangent[group], gate_weight, up_weight, down_weight)
        results.append(jnp.dot(hidden, down_weight, preferred_element_type=jnp.float32).astype(jnp.bfloat16))
        for probe in range(NPROBE):
            tangent = jnp.dot(features, probes[probe], preferred_element_type=jnp.float32)
            weighted = (bending * tangent).astype(jnp.bfloat16)
            curvature = jnp.dot(features.T, weighted, preferred_element_type=jnp.float32)
            total = total + probes[probe].astype(jnp.float32) * curvature
    diag_estimate = total * (1.0 / (NPROBE * GROUPS * TOK))
    return jnp.stack(results), diag_estimate
```

```python
import functools

import jax
import jax.numpy as jnp
from jax import lax
from jax.experimental import pallas as pl
from jax.experimental.pallas import tpu as pltpu
from jax.sharding import PartitionSpec as P


F32, BF16 = jnp.float32, jnp.bfloat16
ANY = pl.BlockSpec(memory_space=pl.ANY)
COLS, HALF = 4, 2


def run_copies(copies):
    for copy in copies:
        copy.start()
    for copy in copies:
        copy.wait()


def partials_body(sizes, at, *refs):
    count = len(sizes)
    sources = refs[:count]
    gate_w, up_w, down_w, probes = refs[count : count + 4]
    acts, right, left, middle, own = refs[count + 4 : count + 9]
    cots, weights, down, total, sems, wsems = refs[count + 9 :]
    step = pl.program_id(0)
    x = at[0]
    quarter = own.shape[1]

    def weight_copy(k):
        source = (gate_w, up_w, probes.at[0], probes.at[1], down_w)[k]
        return pltpu.make_async_copy(source, down if k == 4 else weights.at[k], wsems.at[k])

    def token_copies():
        made = []
        for s, (src, places) in enumerate(zip(sources, sizes)):
            for k, row in enumerate(places):
                for which, into in enumerate((acts, cots)):
                    part = src.at[k, which]
                    sem = sems.at[s, k, which]
                    made.append(pltpu.make_async_copy(part, into.at[pl.ds(row, part.shape[0])], sem))
        return made

    @pl.when(step == 0)
    def _():
        tokens = token_copies()
        for copy in tokens:
            copy.start()
        for k in range(5):
            weight_copy(k).start()
        for copy in tokens:
            copy.wait()

    for k in range(4):
        @pl.when(step == k)
        def _(k=k):
            weight_copy(k).wait()
            total[...] = jnp.dot(acts[...], weights[k], preferred_element_type=F32)

    @pl.when(step == 4)
    def _():
        weight_copy(4).wait()
        total[...] = lax.dot_general(cots[...], down[...], (((1,), (1,)), ((), ())), preferred_element_type=F32)

    def rows(r):
        q = lax.rem(x + r, COLS)
        return pl.ds(pl.multiple_of(q * quarter, 32), quarter)

    half = right.shape[-1]
    lo, hi = slice(0, half), slice(half, 2 * half)
    own[0] = total[rows(0), :]
    right[0, 0] = total[rows(2), lo].astype(BF16)
    right[1, 0] = total[rows(1), hi].astype(BF16)
    left[0, 0] = total[rows(2), hi].astype(BF16)
    left[1, 0] = total[rows(3), lo].astype(BF16)
    middle[0, 0] = total[rows(1), lo]
    middle[1, 0] = total[rows(3), hi]


def partials(x, sources, sizes, gate_w, up_w, down_w, probes):
    shard, width = sources[0].shape[-2:]
    hidden = gate_w.shape[1]
    tokens = shard * sum(len(s) for s in sizes)
    quarter, half = tokens // COLS, hidden // HALF
    message = jax.ShapeDtypeStruct((2, 5, quarter, half), BF16)
    spec = pl.BlockSpec((2, 1, quarter, half), lambda i, at: (0, i, 0, 0))
    return pl.pallas_call(
        functools.partial(partials_body, sizes),
        out_shape=(
            jax.ShapeDtypeStruct((tokens, width), BF16),
            message,
            message,
            jax.ShapeDtypeStruct((2, 5, quarter, half), F32),
            jax.ShapeDtypeStruct((5, quarter, hidden), F32),
        ),
        grid_spec=pltpu.PrefetchScalarGridSpec(
            num_scalar_prefetch=1,
            grid=(5,),
            in_specs=[ANY] * (len(sources) + 4),
            out_specs=(
                pl.BlockSpec((tokens, width), lambda i, at: (0, 0)),
                spec,
                spec,
                spec,
                pl.BlockSpec((1, quarter, hidden), lambda i, at: (i, 0, 0)),
            ),
            scratch_shapes=[
                pltpu.VMEM((tokens, width), BF16),
                pltpu.VMEM((4, width, hidden), BF16),
                pltpu.VMEM((hidden, width), BF16),
                pltpu.VMEM((tokens, hidden), F32),
                pltpu.SemaphoreType.DMA((len(sources), 2, 2)),
                pltpu.SemaphoreType.DMA((5,)),
            ],
        ),
        cost_estimate=pl.CostEstimate(
            flops=10 * tokens * width * hidden,
            transcendentals=0,
            bytes_accessed=10 * width * hidden + 22 * tokens * hidden,
        ),
        name="partials",
    )(x, *sources, gate_w, up_w, down_w, probes)


def terms_body(own, right, left, far_right, far_left, out):
    half = out.shape[-1]
    for h, near, far in ((0, left, far_right), (1, right, far_left)):
        cols = slice(h * half, (h + 1) * half)

        def summed(i):
            return own[i, :, cols] + near[0, i].astype(F32) + far[i].astype(F32)

        gate, up, first, second, error = (summed(i) for i in range(5))
        sigma = 1.0 / (1.0 + jnp.exp(-gate))
        out[h, 0] = (gate * sigma * up).astype(BF16)
        bending = error * up * sigma * (1.0 - sigma) * (2.0 + gate * (1.0 - 2.0 * sigma))
        out[h, 1] = (bending * first).astype(BF16)
        out[h, 2] = (bending * second).astype(BF16)


def terms(own, right, left, far_right, far_left):
    _, quarter, hidden = own.shape
    half, block = hidden // HALF, 32
    near = pl.BlockSpec((1, 5, block, half), lambda i: (1, 0, i, 0))
    far = pl.BlockSpec((5, block, half), lambda i: (0, i, 0))
    return pl.pallas_call(
        terms_body,
        grid=(quarter // block,),
        in_specs=[pl.BlockSpec((5, block, hidden), lambda i: (0, i, 0)), near, near, far, far],
        out_specs=pl.BlockSpec((2, 3, block, half), lambda i: (0, 0, i, 0)),
        out_shape=jax.ShapeDtypeStruct((2, 3, quarter, half), BF16),
        cost_estimate=pl.CostEstimate(
            flops=20 * quarter * hidden, transcendentals=quarter * hidden, bytes_accessed=46 * quarter * hidden
        ),
        name="terms",
    )(own, right, left, far_right, far_left)


def gathered(x, pieces, kinds, into, sems):
    mine, from_left, from_right, far_lo, far_hi = pieces
    quarter, half = mine.shape[-2:]
    copies = []
    for r, part in ((0, mine), (3, from_left), (1, from_right), (2, None)):
        q = lax.rem(x + r, COLS)
        rows = pl.ds(pl.multiple_of(q * quarter, 32), quarter)
        for h in range(HALF):
            for place, kind in enumerate(kinds):
                if part is None:
                    source = (far_lo, far_hi)[h].at[kind]
                else:
                    source = part.at[h, kind]
                copies.append(pltpu.make_async_copy(source, into(h, place, rows), sems.at[r, h, place]))
    return copies


def outputs_body(at, *refs):
    pieces, down, mine, other, hidden, sems = refs[:5], *refs[5:]
    half = pieces[0].shape[-1]

    @pl.when(pl.program_id(0) == 0)
    def _():
        run_copies(gathered(at[0], pieces, (0,), lambda h, k, rows: hidden.at[rows, pl.ds(h * half, half)], sems))

    result = jnp.dot(hidden[...], down[...], preferred_element_type=F32).astype(BF16)
    count = mine.shape[0]
    mine[...] = result[:count]
    other[...] = result[count:]


def outputs_part(x, pieces, down_w):
    quarter, half = pieces[0].shape[-2:]
    tokens, hidden, width = COLS * quarter, HALF * half, down_w.shape[1]
    block = 512
    side = jax.ShapeDtypeStruct((tokens // 2, width), BF16)
    spec = pl.BlockSpec((tokens // 2, block), lambda d, at: (0, d))
    return pl.pallas_call(
        outputs_body,
        out_shape=(side, side),
        grid_spec=pltpu.PrefetchScalarGridSpec(
            num_scalar_prefetch=1,
            grid=(width // block,),
            in_specs=[ANY] * 5 + [pl.BlockSpec((hidden, block), lambda d, at: (0, d))],
            out_specs=(spec, spec),
            scratch_shapes=[pltpu.VMEM((tokens, hidden), BF16), pltpu.SemaphoreType.DMA((4, 2, 1))],
        ),
        cost_estimate=pl.CostEstimate(
            flops=2 * tokens * width * hidden, transcendentals=0, bytes_accessed=2 * width * hidden + 4 * tokens * hidden
        ),
        name="outputs_part",
    )(x, *pieces, down_w)


def curvature_body(scale, final, started, at, *refs):
    pieces, rest = refs[:5], refs[5:]
    if started:
        before, rest = rest[0], rest[1:]
    acts, probes, out, weighted, sems = rest
    half = pieces[0].shape[-1]

    @pl.when((pl.program_id(0) == 0) & (pl.program_id(1) == 0))
    def _():
        run_copies(gathered(at[0], pieces, (1, 2), lambda h, k, rows: weighted.at[h, rows, pl.ds(k * half, half)], sems))

    h = lax.rem(at[1] + pl.program_id(0), HALF)
    both = lax.dot_general(acts[...], weighted[h], (((0,), (0,)), ((), ())), preferred_element_type=F32)
    total = probes[0].astype(F32) * both[:, :half] + probes[1].astype(F32) * both[:, half:]
    if started:
        total = total + before[0]
    if final:
        out[...] = (total * scale).astype(out.dtype)
    else:
        out[0] = total


def curvature(x_and_half, pieces, before, acts, probes, scale=1.0, halves=HALF, final=None):
    quarter, half = pieces[0].shape[-2:]
    tokens, width = acts.shape
    block = 256
    which = lambda g, d, at: (lax.rem(at[1] + g, HALF), d, 0)
    per_half = pl.BlockSpec((1, block, half), which)
    started = before is not None
    return pl.pallas_call(
        functools.partial(curvature_body, scale, final is not None, started),
        out_shape=(
            jax.ShapeDtypeStruct((HALF, width, half), F32)
            if final is None
            else jax.ShapeDtypeStruct((width, half), final)
        ),
        grid_spec=pltpu.PrefetchScalarGridSpec(
            num_scalar_prefetch=1,
            grid=(halves, width // block),
            in_specs=[ANY] * 5
            + ([per_half] if started else [])
            + [
                pl.BlockSpec((tokens, block), lambda g, d, at: (0, d)),
                pl.BlockSpec((2, block, half), lambda g, d, at: (0, d, lax.rem(at[1] + g, HALF))),
            ],
            out_specs=per_half if final is None else pl.BlockSpec((block, half), lambda g, d, at: (d, 0)),
            scratch_shapes=[pltpu.VMEM((HALF, tokens, 2 * half), BF16), pltpu.SemaphoreType.DMA((4, 2, 2))],
        ),
        cost_estimate=pl.CostEstimate(
            flops=4 * tokens * width * half * halves, transcendentals=0, bytes_accessed=12 * width * half * halves
        ),
        name="curvature",
    )(x_and_half, *pieces, *((before,) if started else ()), acts, probes)


def moved(axis, to):
    size = lax.axis_size(axis)
    pairs = [(i, to(i) % size) for i in range(size)]
    return lambda value: lax.ppermute(value, axis, pairs)


def local(activations, cotangent, gate_w, up_w, down_w, probes):
    shard, width = activations.shape[1:]
    rows = lax.axis_size("row")
    z_step = 4
    partner = moved("row", lambda i: i ^ 1)
    across = moved("row", lambda i: i ^ 2)
    z_up, z_down = moved("row", lambda i: i + z_step), moved("row", lambda i: i - z_step)
    z_far = moved("row", lambda i: i + 2 * z_step)
    x_up, x_down = moved("col", lambda i: i + 1), moved("col", lambda i: i - 1)
    other_group = moved("dp", lambda i: i + 1)

    col, group = lax.axis_index("col"), lax.axis_index("dp")
    x = jnp.stack([col, jnp.zeros_like(col)]).astype(jnp.int32)
    x_other = jnp.stack([col, 1 - group]).astype(jnp.int32)
    x_mine = jnp.stack([col, group]).astype(jnp.int32)
    weights = (gate_w, up_w, down_w, probes)

    mine = jnp.concatenate([activations, cotangent], axis=0)
    near = jnp.stack([mine, across(mine)])
    from_below, from_above = z_up(near), z_down(near)
    near_partner = partner(near)
    far_own, far_across = z_up(from_below[0]), z_down(from_above[1])
    below_partner, above_partner = partner(from_below), partner(from_above)
    far_own, far_across = far_own[None], far_across[None]
    far_own_partner, far_across_partner = partner(far_own), partner(far_across)

    s = shard
    chunks = (
        ((near, near_partner), ((0, s), (2 * s, 3 * s))),
        (
            (from_below, from_above, below_partner, above_partner),
            ((0, 2 * s), (s, 3 * s), (4 * s, 6 * s), (5 * s, 7 * s)),
        ),
        (
            (far_own, far_across, far_own_partner, far_across_partner),
            ((0,), (s,), (2 * s,), (3 * s,)),
        ),
    )

    def ring_sum(sources, sizes):
        acts, right, left, middle, own = partials(x, sources, sizes, *weights)
        right, left = x_up(right), x_down(left)
        far_right = x_up((middle[0] + right[0].astype(F32)).astype(BF16))
        far_left = x_down((middle[1] + left[0].astype(F32)).astype(BF16))
        return acts, terms(own, right, left, far_right, far_left)

    def ring_gather(piece):
        from_left, from_right = x_up(piece), x_down(piece)
        return piece, from_left, from_right, x_up(from_left[0]), x_down(from_right[1])

    acts0, piece0 = ring_sum(*chunks[0])
    acts1, piece1 = ring_sum(*chunks[1])
    pieces0 = ring_gather(piece0)
    acts2, piece2 = ring_sum(*chunks[2])
    pieces1 = ring_gather(piece1)
    pieces2 = ring_gather(piece2)

    scale = 1.0 / (probes.shape[0] * lax.axis_size("dp") * shard * rows)

    def halves_summed(pieces):
        kept, sent = outputs_part(x, pieces, down_w)
        return kept.astype(F32) + partner(sent).astype(F32)

    near_sum = halves_summed(pieces0).reshape(2, s, width)
    total = curvature(x, pieces0, None, acts0, probes)
    side_sum = halves_summed(pieces1).reshape(2, 2, s, width)
    from_up = z_down(side_sum[:, 0].astype(BF16))
    from_down = z_up(side_sum[:, 1].astype(BF16))
    total = curvature(x, pieces1, total, acts1, probes)
    near_sum = near_sum + from_up.astype(F32) + from_down.astype(F32)
    near_sum = near_sum[0] + across(near_sum[1].astype(BF16)).astype(F32)

    far_sum = halves_summed(pieces2).reshape(2, s, width)
    far_sum = far_sum[0] + across(far_sum[1].astype(BF16)).astype(F32)
    sent = curvature(x_other, pieces2, total, acts2, probes, scale, 1, BF16)
    arrived = other_group(sent)
    kept = curvature(x_mine, pieces2, total, acts2, probes, scale, 1, F32)
    outputs = near_sum + z_far(far_sum.astype(BF16)).astype(F32)
    return outputs.astype(BF16)[None], kept + arrived.astype(F32)


def solution(mesh):
    in_specs = (
        P("dp", "row", "col"),
        P("dp", "row", "col"),
        P("col", "row"),
        P("col", "row"),
        P("row", "col"),
        P(None, "col", "row"),
    )
    out_specs = (P("dp", "row", "col"), P("col", ("row", "dp")))
    return jax.shard_map(local, mesh=mesh, in_specs=in_specs, out_specs=out_specs, check_vma=False)
```

```python
import functools

import jax
import jax.numpy as jnp
from jax import lax
from jax.experimental import pallas as pl
from jax.experimental.pallas import tpu as pltpu
from jax.sharding import PartitionSpec as P


F32, BF16 = jnp.float32, jnp.bfloat16
HBM = pl.BlockSpec(memory_space=pltpu.MemorySpace.HBM)
COLS, HALF = 4, 2


def run_copies(copies):
    for copy in copies:
        copy.start()
    for copy in copies:
        copy.wait()


def pack_body(acts, cots, out, sems):
    run_copies(
        [pltpu.make_async_copy(acts.at[0], out.at[0], sems.at[0]), pltpu.make_async_copy(cots.at[0], out.at[1], sems.at[1])]
    )


def pack(acts, cots):
    return pl.pallas_call(
        pack_body,
        in_specs=[HBM, HBM],
        out_specs=HBM,
        out_shape=jax.ShapeDtypeStruct((2, *acts.shape[1:]), acts.dtype),
        scratch_shapes=[pltpu.SemaphoreType.DMA((2,))],
        name="pack",
    )(acts, cots)


def partials_body(count, at, *refs):
    sources = refs[:count]
    gate_w, up_w, down_w, probes = refs[count : count + 4]
    acts_out, right, left, middle, own = refs[count + 4 : count + 9]
    acts, cots, weights, down, total, rights, lefts, middles, owns, sems, wsems, osems, asem = refs[count + 9 :]
    x = at[0]
    quarter, shard = own.shape[1], sources[0].shape[1]
    half = right.shape[-1]
    lo, hi = slice(0, half), slice(half, 2 * half)

    tokens = [
        [
            pltpu.make_async_copy(src.at[which], into.at[pl.ds(s * shard, shard)], sems.at[which, s])
            for s, src in enumerate(sources)
        ]
        for which, into in enumerate((acts, cots))
    ]
    loads = [
        pltpu.make_async_copy(src, into, wsems.at[k])
        for k, (src, into) in enumerate(
            (
                (gate_w, weights.at[0]),
                (up_w, weights.at[1]),
                (probes.at[0], weights.at[2]),
                (probes.at[1], weights.at[3]),
                (down_w, down),
            )
        )
    ]
    for copy in tokens[0]:
        copy.start()
    for copy in loads[:2]:
        copy.start()
    for copy in tokens[1]:
        copy.start()
    for copy in loads[2:]:
        copy.start()
    for copy in tokens[0]:
        copy.wait()
    keep = pltpu.make_async_copy(acts, acts_out, asem)
    keep.start()

    def rows(r):
        return pl.ds(pl.multiple_of(lax.rem(x + r, COLS) * quarter, 32), quarter)

    stores = []
    for k in range(5):
        loads[k].wait()
        part = total.at[k % 2]
        if k < 4:
            part[...] = jnp.dot(acts[...], weights[k], preferred_element_type=F32)
        else:
            for copy in tokens[1]:
                copy.wait()
            part[...] = lax.dot_general(cots[...], down[...], (((1,), (1,)), ((), ())), preferred_element_type=F32)
        rights[0, k] = part[rows(2), lo].astype(BF16)
        rights[1, k] = part[rows(1), hi].astype(BF16)
        lefts[0, k] = part[rows(2), hi].astype(BF16)
        lefts[1, k] = part[rows(3), lo].astype(BF16)
        middles[0, k] = part[rows(1), lo]
        middles[1, k] = part[rows(3), hi]
        owns[k] = part[rows(0), :]
        moves = [(owns.at[k], own.at[k])]
        for held, into in ((rights, right), (lefts, left), (middles, middle)):
            moves += [(held.at[side, k], into.at[side, k]) for side in range(2)]
        for n, (held, into) in enumerate(moves):
            copy = pltpu.make_async_copy(held, into, osems.at[k, n])
            copy.start()
            stores.append(copy)
    for copy in stores:
        copy.wait()
    keep.wait()


def partials(x, sources, gate_w, up_w, down_w, probes):
    shard, width = sources[0].shape[1:]
    hidden = gate_w.shape[1]
    tokens = shard * len(sources)
    quarter, half = tokens // COLS, hidden // HALF
    shapes = [
        ((tokens, width), BF16),
        ((2, 5, quarter, half), BF16),
        ((2, 5, quarter, half), BF16),
        ((2, 5, quarter, half), F32),
        ((5, quarter, hidden), F32),
    ]
    return pl.pallas_call(
        functools.partial(partials_body, len(sources)),
        out_shape=tuple(jax.ShapeDtypeStruct(*shape) for shape in shapes),
        grid_spec=pltpu.PrefetchScalarGridSpec(
            num_scalar_prefetch=1,
            grid=(),
            in_specs=[HBM] * (len(sources) + 4),
            out_specs=(HBM,) * 5,
            scratch_shapes=[
                pltpu.VMEM((tokens, width), BF16),
                pltpu.VMEM((tokens, width), BF16),
                pltpu.VMEM((4, width, hidden), BF16),
                pltpu.VMEM((hidden, width), BF16),
                pltpu.VMEM((2, tokens, hidden), F32),
                *(pltpu.VMEM(*shape) for shape in shapes[1:]),
                pltpu.SemaphoreType.DMA((2, len(sources))),
                pltpu.SemaphoreType.DMA((5,)),
                pltpu.SemaphoreType.DMA((5, 7)),
                pltpu.SemaphoreType.DMA,
            ],
        ),
        cost_estimate=pl.CostEstimate(
            flops=10 * tokens * width * hidden,
            transcendentals=0,
            bytes_accessed=10 * width * hidden + 22 * tokens * hidden,
        ),
        name="partials",
    )(x, *sources, gate_w, up_w, down_w, probes)


def terms_body(own, right, left, far_right, far_left, *outs):
    half = outs[0].shape[-1]
    for h, near, far in ((0, left, far_right), (1, right, far_left)):
        cols = slice(h * half, (h + 1) * half)

        def summed(i):
            return own[i, :, cols] + near[0, i].astype(F32) + far[i].astype(F32)

        gate, up, first, second, error = (summed(i) for i in range(5))
        sigma = 1.0 / (1.0 + jnp.exp(-gate))
        bending = error * up * sigma * (1.0 - sigma) * (2.0 + gate * (1.0 - 2.0 * sigma))
        values = (gate * sigma * up, bending * first, bending * second)
        places = [out.at[h, k] for out in outs for k in range(out.shape[1])]
        for place, value in zip(places, values):
            place[...] = value.astype(BF16)


def terms(own, right, left, far_right, far_left, kinds):
    _, quarter, hidden = own.shape
    half, block = hidden // HALF, 96
    near = pl.BlockSpec((1, 5, block, half), lambda i: (1, 0, i, 0))
    far = pl.BlockSpec((5, block, half), lambda i: (0, i, 0))
    return pl.pallas_call(
        terms_body,
        grid=(quarter // block,),
        in_specs=[pl.BlockSpec((5, block, hidden), lambda i: (0, i, 0)), near, near, far, far],
        out_specs=[pl.BlockSpec((2, n, block, half), lambda i: (0, 0, i, 0)) for n in kinds],
        out_shape=[jax.ShapeDtypeStruct((2, n, quarter, half), BF16) for n in kinds],
        cost_estimate=pl.CostEstimate(
            flops=20 * quarter * hidden, transcendentals=quarter * hidden, bytes_accessed=46 * quarter * hidden
        ),
        name="terms",
    )(own, right, left, far_right, far_left)


def gathered(x, pieces, kinds, into, sems):
    mine, from_left, from_right, far_lo, far_hi = pieces
    quarter, _ = mine.shape[-2:]
    copies = []
    for r, parts in ((0, (mine, mine)), (3, (from_left,) * 2), (1, (from_right,) * 2), (2, (far_lo, far_hi))):
        q = lax.rem(x + r, COLS)
        rows = pl.ds(pl.multiple_of(q * quarter, 32), quarter)
        for h, part in enumerate(parts):
            for place, kind in enumerate(kinds):
                source = part.at[h, kind] if len(part.shape) == 4 else part.at[kind]
                copies.append(pltpu.make_async_copy(source, into(h, place, rows), sems.at[r, h, place]))
    return copies


def outputs_body(kind, at, *refs):
    pieces, down, kept, sent, hidden, sems = refs[:5], *refs[5:]
    half = pieces[0].shape[-1]

    @pl.when(pl.program_id(0) == 0)
    def _():
        run_copies(gathered(at[0], pieces, (kind,), lambda h, k, rows: hidden.at[rows, pl.ds(h * half, half)], sems))

    result = jnp.dot(hidden[...], down[...], preferred_element_type=F32)
    count = kept.shape[0]
    kept[...] = result[:count]
    sent[...] = result[count:]


def outputs_part(x, pieces, down_w, kind=0):
    quarter, half = pieces[0].shape[-2:]
    tokens, hidden, width = COLS * quarter, HALF * half, down_w.shape[1]
    block = 512
    side = jax.ShapeDtypeStruct((tokens // 2, width), F32)
    spec = pl.BlockSpec((tokens // 2, block), lambda d, at: (0, d))
    return pl.pallas_call(
        functools.partial(outputs_body, kind),
        out_shape=(side, side),
        grid_spec=pltpu.PrefetchScalarGridSpec(
            num_scalar_prefetch=1,
            grid=(width // block,),
            in_specs=[HBM] * 5 + [pl.BlockSpec((hidden, block), lambda d, at: (0, d))],
            out_specs=(spec, spec),
            scratch_shapes=[pltpu.VMEM((tokens, hidden), BF16), pltpu.SemaphoreType.DMA((4, 2, 1))],
        ),
        cost_estimate=pl.CostEstimate(
            flops=2 * tokens * width * hidden, transcendentals=0, bytes_accessed=2 * width * hidden + 4 * tokens * hidden
        ),
        name="outputs_part",
    )(x, *pieces, down_w)


def curvature_body(kinds, at, *refs):
    pieces, acts, probes, out, weighted, sems = refs[:5], *refs[5:]
    half = pieces[0].shape[-1]

    @pl.when(pl.program_id(0) == 0)
    def _():
        place = lambda h, k, rows: weighted.at[rows, pl.ds((2 * h + k) * half, half)]
        run_copies(gathered(at[0], pieces, kinds, place, sems))

    both = lax.dot_general(acts[...], weighted[...], (((0,), (0,)), ((), ())), preferred_element_type=F32)
    for h in range(HALF):
        cols = slice(h * half, (h + 1) * half)
        first, second = (both[:, (2 * h + k) * half : (2 * h + k + 1) * half] for k in range(2))
        out[h] = probes[0, :, cols].astype(F32) * first + probes[1, :, cols].astype(F32) * second


def curvature(x, pieces, kinds, acts, probes):
    _, half = pieces[0].shape[-2:]
    tokens, width = acts.shape
    hidden, block = HALF * half, 256
    return pl.pallas_call(
        functools.partial(curvature_body, kinds),
        out_shape=jax.ShapeDtypeStruct((HALF, width, half), F32),
        grid_spec=pltpu.PrefetchScalarGridSpec(
            num_scalar_prefetch=1,
            grid=(width // block,),
            in_specs=[HBM] * 5
            + [
                pl.BlockSpec((tokens, block), lambda d, at: (0, d)),
                pl.BlockSpec((2, block, hidden), lambda d, at: (0, d, 0)),
            ],
            out_specs=pl.BlockSpec((HALF, block, half), lambda d, at: (0, d, 0)),
            scratch_shapes=[pltpu.VMEM((tokens, 2 * hidden), BF16), pltpu.SemaphoreType.DMA((4, 2, 2))],
        ),
        cost_estimate=pl.CostEstimate(
            flops=4 * tokens * width * hidden, transcendentals=0, bytes_accessed=12 * width * hidden
        ),
        name="curvature",
    )(x, *pieces, acts, probes)


def final_body(kinds, scale, at, *refs):
    pieces, before, acts, probes, out, weighted, sems = refs[:5], *refs[5:]
    half = pieces[0].shape[-1]
    wanted = at[1]

    @pl.when(pl.program_id(0) == 0)
    def _():
        place = lambda h, k, rows: weighted.at[h, rows, pl.ds(k * half, half)]
        copies = gathered(at[0], pieces, kinds, place, sems)
        for ready in (True, False):
            for n, copy in enumerate(copies):
                h = (n // len(kinds)) % HALF

                @pl.when(wanted == h)
                def _(copy=copy):
                    (copy.start if ready else copy.wait)()

    both = lax.dot_general(acts[...], weighted[wanted], (((0,), (0,)), ((), ())), preferred_element_type=F32)
    total = probes[0].astype(F32) * both[:, :half] + probes[1].astype(F32) * both[:, half:]
    out[...] = ((total + before[0]) * scale).astype(out.dtype)


def final_curvature(x_and_half, pieces, kinds, before, acts, probes, scale, dtype):
    _, half = pieces[0].shape[-2:]
    tokens, width = acts.shape
    block = 512
    return pl.pallas_call(
        functools.partial(final_body, kinds, scale),
        out_shape=jax.ShapeDtypeStruct((width, half), dtype),
        grid_spec=pltpu.PrefetchScalarGridSpec(
            num_scalar_prefetch=1,
            grid=(width // block,),
            in_specs=[HBM] * 5
            + [
                pl.BlockSpec((1, block, half), lambda d, at: (at[1], d, 0)),
                pl.BlockSpec((tokens, block), lambda d, at: (0, d)),
                pl.BlockSpec((2, block, half), lambda d, at: (0, d, at[1])),
            ],
            out_specs=pl.BlockSpec((block, half), lambda d, at: (d, 0)),
            scratch_shapes=[pltpu.VMEM((HALF, tokens, 2 * half), BF16), pltpu.SemaphoreType.DMA((4, 2, 2))],
        ),
        cost_estimate=pl.CostEstimate(
            flops=4 * tokens * width * half, transcendentals=0, bytes_accessed=12 * width * half
        ),
        name="final_curvature",
    )(x_and_half, *pieces, before, acts, probes)


def moved(axis, to):
    size = lax.axis_size(axis)
    pairs = [(i, to(i) % size) for i in range(size)]
    return lambda value: lax.ppermute(value, axis, pairs)


def program(activations, cotangent, gate_w, up_w, down_w, probes):
    s, width = activations.shape[1:]
    rows = lax.axis_size("row")
    z_step = 4
    partner = moved("row", lambda i: i ^ 1)
    across = moved("row", lambda i: i ^ 2)
    z_up, z_down = moved("row", lambda i: i + z_step), moved("row", lambda i: i - z_step)
    z_far = moved("row", lambda i: i + 2 * z_step)
    x_up, x_down = moved("col", lambda i: i + 1), moved("col", lambda i: i - 1)
    x_far = moved("col", lambda i: i + 2)
    other_group = moved("dp", lambda i: i + 1)

    col, group = lax.axis_index("col"), lax.axis_index("dp")
    x = jnp.stack([col, jnp.zeros_like(col)]).astype(jnp.int32)
    x_other = jnp.stack([col, 1 - group]).astype(jnp.int32)
    x_mine = jnp.stack([col, group]).astype(jnp.int32)
    weights = (gate_w, up_w, down_w, probes)

    mine = pack(activations, cotangent)
    beside = across(mine)
    below, above = z_up(mine), z_down(mine)
    first = [mine, beside, below, above]
    first += [partner(part) for part in first]
    below_beside, above_beside = z_up(beside), z_down(beside)
    opposite, opposite_beside = z_up(below), z_down(above_beside)
    second = [below_beside, above_beside, opposite, opposite_beside]
    second += [partner(part) for part in second]

    def ring_start(sources):
        acts, right, left, middle, own = partials(x, sources, *weights)
        return acts, x_up(right), x_down(left), middle, own

    def ring_sum(right, left, middle, own, kinds):
        far_right = x_up((middle[0] + right[0].astype(F32)).astype(BF16))
        far_left = x_down((middle[1] + left[0].astype(F32)).astype(BF16))
        return terms(own, right, left, far_right, far_left, kinds)

    def ring_gather(piece):
        from_left, from_right = x_up(piece), x_down(piece)
        far_left, far_right = x_up(from_left[0]), x_down(from_right[1])
        return piece, from_left, from_right, far_left, far_right

    acts_a, right_a, left_a, middle_a, own_a = ring_start(first)
    acts_b, right_b, left_b, middle_b, own_b = ring_start(second)
    (piece_a,) = ring_sum(right_a, left_a, middle_a, own_a, (3,))
    pieces_a = ring_gather(piece_a)
    hidden_b, weighted_b = ring_sum(right_b, left_b, middle_b, own_b, (1, 2))
    far_b = x_far(hidden_b)
    hiddens_b = (hidden_b, x_up(hidden_b), x_down(hidden_b), far_b, far_b)
    weighteds_b = ring_gather(weighted_b)

    def halves_summed(pieces):
        kept, sent = outputs_part(x, pieces, down_w)
        return (kept + partner(sent)).reshape(4, s, width)

    sum_a = halves_summed(pieces_a)
    from_above, from_below = z_down(sum_a[2].astype(BF16)), z_up(sum_a[3].astype(BF16))
    total = curvature(x, pieces_a, (1, 2), acts_a, probes)

    sum_b = halves_summed(hiddens_b)
    near = sum_a[0] + from_above.astype(F32) + from_below.astype(F32)
    from_far = z_far(sum_b[2:].astype(BF16))
    beside_above, beside_below = z_down(sum_b[0].astype(BF16)), z_up(sum_b[1].astype(BF16))
    near = near + from_far[0].astype(F32)
    other = sum_a[1] + beside_above.astype(F32) + beside_below.astype(F32) + from_far[1].astype(F32)
    outputs = near + across(other.astype(BF16)).astype(F32)

    scale = 1.0 / (probes.shape[0] * lax.axis_size("dp") * s * rows)
    sent = final_curvature(x_other, weighteds_b, (0, 1), total, acts_b, probes, scale, BF16)
    arrived = other_group(sent)
    kept = final_curvature(x_mine, weighteds_b, (0, 1), total, acts_b, probes, scale, F32)
    return outputs.astype(BF16)[None], kept + arrived.astype(F32)


def solution(mesh):
    in_specs = (
        P("dp", "row", "col"),
        P("dp", "row", "col"),
        P("col", "row"),
        P("col", "row"),
        P("row", "col"),
        P(None, "col", "row"),
    )
    out_specs = (P("dp", "row", "col"), P("col", ("row", "dp")))
    return jax.shard_map(program, mesh=mesh, in_specs=in_specs, out_specs=out_specs, check_vma=False)
```

```python
import functools

import jax
import jax.numpy as jnp
from jax import lax
from jax.experimental import pallas as pl
from jax.experimental.pallas import tpu as pltpu
from jax.sharding import PartitionSpec as P


F32, BF16 = jnp.float32, jnp.bfloat16
ANY = pl.BlockSpec(memory_space=pl.ANY)
HBM = pl.BlockSpec(memory_space=pltpu.MemorySpace.HBM)
COLS, HALF = 4, 2


def grant(mebibytes):
    return pltpu.CompilerParams(vmem_limit_bytes=mebibytes << 20)


def run_copies(copies):
    for copy in copies:
        copy.start()
    for copy in copies:
        copy.wait()


def pack_body(acts, cots, out, sems):
    run_copies([pltpu.make_async_copy(part.at[0], out.at[k], sems.at[k]) for k, part in enumerate((acts, cots))])


def pack(acts, cots):
    return pl.pallas_call(
        pack_body,
        in_specs=[HBM, HBM],
        out_shape=jax.ShapeDtypeStruct((2, *acts.shape[1:]), acts.dtype),
        scratch_shapes=[pltpu.SemaphoreType.DMA((2,))],
        compiler_params=grant(4),
        name="pack",
    )(acts, cots)


def partials_body(count, at, *refs):
    sources = refs[:count]
    gate_w, up_w, down_w, probes = refs[count : count + 4]
    acts_out, right, left, middle, own = refs[count + 4 : count + 9]
    acts, cots, weights, down, total, rights, lefts, middles, owns, sems, wsems, osems, asem = refs[count + 9 :]
    x = at[0]
    quarter, shard = own.shape[1], sources[0].shape[1]
    half = right.shape[-1]
    lo, hi = slice(0, half), slice(half, 2 * half)

    tokens = [
        [
            pltpu.make_async_copy(src.at[which], into.at[pl.ds(s * shard, shard)], sems.at[which, s])
            for s, src in enumerate(sources)
        ]
        for which, into in enumerate((acts, cots))
    ]
    loads = [
        pltpu.make_async_copy(src, into, wsems.at[k])
        for k, (src, into) in enumerate(
            (
                (gate_w, weights.at[0]),
                (up_w, weights.at[1]),
                (probes.at[0], weights.at[2]),
                (probes.at[1], weights.at[3]),
                (down_w, down),
            )
        )
    ]
    for copy in tokens[0]:
        copy.start()
    for copy in loads[:2]:
        copy.start()
    for copy in tokens[1]:
        copy.start()
    for copy in loads[2:]:
        copy.start()
    for copy in tokens[0]:
        copy.wait()
    keep = pltpu.make_async_copy(acts, acts_out, asem)
    keep.start()

    def rows(r):
        return pl.ds(pl.multiple_of(lax.rem(x + r, COLS) * quarter, 32), quarter)

    stores = []
    for k in range(5):
        loads[k].wait()
        part = total.at[k % 2]
        if k < 4:
            part[...] = jnp.dot(acts[...], weights[k], preferred_element_type=F32)
        else:
            for copy in tokens[1]:
                copy.wait()
            part[...] = lax.dot_general(cots[...], down[...], (((1,), (1,)), ((), ())), preferred_element_type=F32)
        rights[0, k] = part[rows(2), lo].astype(BF16)
        rights[1, k] = part[rows(1), hi].astype(BF16)
        lefts[0, k] = part[rows(2), hi].astype(BF16)
        lefts[1, k] = part[rows(3), lo].astype(BF16)
        middles[0, k] = part[rows(1), lo]
        middles[1, k] = part[rows(3), hi]
        owns[k] = part[rows(0), :]
        moves = [(owns.at[k], own.at[k])]
        for held, into in ((rights, right), (lefts, left), (middles, middle)):
            moves += [(held.at[side, k], into.at[side, k]) for side in range(2)]
        for n, (held, into) in enumerate(moves):
            copy = pltpu.make_async_copy(held, into, osems.at[k, n])
            copy.start()
            stores.append(copy)
    for copy in stores:
        copy.wait()
    keep.wait()


def partials(x, sources, gate_w, up_w, down_w, probes):
    shard, width = sources[0].shape[1:]
    hidden = gate_w.shape[1]
    tokens = shard * len(sources)
    quarter, half = tokens // COLS, hidden // HALF
    shapes = [
        ((tokens, width), BF16),
        ((2, 5, quarter, half), BF16),
        ((2, 5, quarter, half), BF16),
        ((2, 5, quarter, half), F32),
        ((5, quarter, hidden), F32),
    ]
    return pl.pallas_call(
        functools.partial(partials_body, len(sources)),
        out_shape=tuple(jax.ShapeDtypeStruct(*shape) for shape in shapes),
        grid_spec=pltpu.PrefetchScalarGridSpec(
            num_scalar_prefetch=1,
            grid=(),
            in_specs=[ANY] * len(sources) + [HBM] * 4,
            out_specs=(ANY,) * 5,
            scratch_shapes=[
                pltpu.VMEM((tokens, width), BF16),
                pltpu.VMEM((tokens, width), BF16),
                pltpu.VMEM((4, width, hidden), BF16),
                pltpu.VMEM((hidden, width), BF16),
                pltpu.VMEM((2, tokens, hidden), F32),
                *(pltpu.VMEM(*shape) for shape in shapes[1:]),
                pltpu.SemaphoreType.DMA((2, len(sources))),
                pltpu.SemaphoreType.DMA((5,)),
                pltpu.SemaphoreType.DMA((5, 7)),
                pltpu.SemaphoreType.DMA,
            ],
        ),
        cost_estimate=pl.CostEstimate(
            flops=10 * tokens * width * hidden,
            transcendentals=0,
            bytes_accessed=10 * width * hidden + 22 * tokens * hidden,
        ),
        compiler_params=grant(24),
        name="partials",
    )(x, *sources, gate_w, up_w, down_w, probes)


def terms_body(own, right, left, far_right, far_left, *outs):
    half, block = outs[0].shape[-1], 32
    places = [(out, k) for out in outs for k in range(out.shape[1])]

    def some_rows(n, carry):
        rows = pl.ds(pl.multiple_of(n * block, block), block)
        for h, near, far in ((0, left, far_right), (1, right, far_left)):
            cols = slice(h * half, (h + 1) * half)

            def summed(i):
                return own[i, rows, cols] + near[1, i, rows].astype(F32) + far[i, rows].astype(F32)

            gate, up, first, second, error = (summed(i) for i in range(5))
            sigma = 1.0 / (1.0 + jnp.exp(-gate))
            bending = error * up * sigma * (1.0 - sigma) * (2.0 + gate * (1.0 - 2.0 * sigma))
            values = (gate * sigma * up, bending * first, bending * second)
            for (out, k), value in zip(places, values):
                out[h, k, rows] = value.astype(BF16)
        return carry

    lax.fori_loop(0, own.shape[1] // block, some_rows, 0)


def terms(own, right, left, far_right, far_left, kinds):
    _, quarter, hidden = own.shape
    half = hidden // HALF
    return pl.pallas_call(
        terms_body,
        out_shape=[jax.ShapeDtypeStruct((2, n, quarter, half), BF16) for n in kinds],
        cost_estimate=pl.CostEstimate(
            flops=20 * quarter * hidden, transcendentals=quarter * hidden, bytes_accessed=46 * quarter * hidden
        ),
        compiler_params=grant(12),
        name="terms",
    )(own, right, left, far_right, far_left)


def flip_body(acts, out):
    out[...] = acts[...].T


def flip(acts):
    tokens, width = acts.shape
    block = 256
    return pl.pallas_call(
        flip_body,
        grid=(width // block,),
        in_specs=[pl.BlockSpec((tokens, block), lambda d: (0, d))],
        out_specs=pl.BlockSpec((block, tokens), lambda d: (d, 0)),
        out_shape=jax.ShapeDtypeStruct((width, tokens), acts.dtype),
        compiler_params=grant(12),
        name="flip",
    )(acts)


def gathered(x, pieces, kinds, into, sems):
    mine, from_left, from_right, far_lo, far_hi = pieces
    quarter, _ = mine.shape[-2:]
    copies = []
    for r, parts in ((0, (mine, mine)), (3, (from_left,) * 2), (1, (from_right,) * 2), (2, (far_lo, far_hi))):
        q = lax.rem(x + r, COLS)
        rows = pl.ds(pl.multiple_of(q * quarter, 32), quarter)
        for h, part in enumerate(parts):
            for place, kind in enumerate(kinds):
                source = part.at[h, kind] if len(part.shape) == 4 else part.at[kind]
                copies.append(pltpu.make_async_copy(source, into(h, place, rows), sems.at[r, h, place]))
    return copies


def outputs_body(kind, at, *refs):
    pieces, down, kept, sent, hidden, sems = refs[:5], *refs[5:]
    half = pieces[0].shape[-1]

    @pl.when(pl.program_id(0) == 0)
    def _():
        run_copies(gathered(at[0], pieces, (kind,), lambda h, k, rows: hidden.at[rows, pl.ds(h * half, half)], sems))

    result = jnp.dot(hidden[...], down[...], preferred_element_type=F32)
    count = kept.shape[0]
    kept[...] = result[:count]
    sent[...] = result[count:]


def outputs_part(x, pieces, down_w, kind=0):
    quarter, half = pieces[0].shape[-2:]
    tokens, hidden, width = COLS * quarter, HALF * half, down_w.shape[1]
    block = 512
    side = jax.ShapeDtypeStruct((tokens // 2, width), F32)
    spec = pl.BlockSpec((tokens // 2, block), lambda d, at: (0, d))
    return pl.pallas_call(
        functools.partial(outputs_body, kind),
        out_shape=(side, side),
        grid_spec=pltpu.PrefetchScalarGridSpec(
            num_scalar_prefetch=1,
            grid=(width // block,),
            in_specs=[ANY] * 5 + [pl.BlockSpec((hidden, block), lambda d, at: (0, d))],
            out_specs=(spec, spec),
            scratch_shapes=[pltpu.VMEM((tokens, hidden), BF16), pltpu.SemaphoreType.DMA((4, 2, 1))],
        ),
        cost_estimate=pl.CostEstimate(
            flops=2 * tokens * width * hidden, transcendentals=0, bytes_accessed=2 * width * hidden + 4 * tokens * hidden
        ),
        compiler_params=grant(12),
        name="outputs_part",
    )(x, *pieces, down_w)


def curvature_body(kinds, at, *refs):
    pieces, acts, probes, out, weighted, sems = refs[:5], *refs[5:]
    half = pieces[0].shape[-1]

    @pl.when(pl.program_id(0) == 0)
    def _():
        place = lambda h, k, rows: weighted.at[rows, pl.ds((2 * h + k) * half, half)]
        run_copies(gathered(at[0], pieces, kinds, place, sems))

    both = jnp.dot(acts[...], weighted[...], preferred_element_type=F32)
    for h in range(HALF):
        cols = slice(h * half, (h + 1) * half)
        first, second = (both[:, (2 * h + k) * half : (2 * h + k + 1) * half] for k in range(2))
        out[h] = probes[0, :, cols].astype(F32) * first + probes[1, :, cols].astype(F32) * second


def curvature(x, pieces, kinds, acts, probes):
    _, half = pieces[0].shape[-2:]
    width, tokens = acts.shape
    hidden, block = HALF * half, 256
    return pl.pallas_call(
        functools.partial(curvature_body, kinds),
        out_shape=jax.ShapeDtypeStruct((HALF, width, half), F32),
        grid_spec=pltpu.PrefetchScalarGridSpec(
            num_scalar_prefetch=1,
            grid=(width // block,),
            in_specs=[ANY] * 5
            + [
                pl.BlockSpec((block, tokens), lambda d, at: (d, 0)),
                pl.BlockSpec((2, block, hidden), lambda d, at: (0, d, 0)),
            ],
            out_specs=pl.BlockSpec((HALF, block, half), lambda d, at: (0, d, 0)),
            scratch_shapes=[pltpu.VMEM((tokens, 2 * hidden), BF16), pltpu.SemaphoreType.DMA((4, 2, 2))],
        ),
        cost_estimate=pl.CostEstimate(
            flops=4 * tokens * width * hidden, transcendentals=0, bytes_accessed=12 * width * hidden
        ),
        compiler_params=grant(16),
        name="curvature",
    )(x, *pieces, acts, probes)


def final_body(kinds, scale, at, *refs):
    pieces, before, acts, probes, out, weighted, sems = refs[:5], *refs[5:]
    half = pieces[0].shape[-1]
    wanted = at[1]

    @pl.when(pl.program_id(0) == 0)
    def _():
        place = lambda h, k, rows: weighted.at[h, rows, pl.ds(k * half, half)]
        copies = gathered(at[0], pieces, kinds, place, sems)
        for ready in (True, False):
            for n, copy in enumerate(copies):
                h = (n // len(kinds)) % HALF

                @pl.when(wanted == h)
                def _(copy=copy):
                    (copy.start if ready else copy.wait)()

    both = jnp.dot(acts[...], weighted[wanted], preferred_element_type=F32)
    total = probes[0].astype(F32) * both[:, :half] + probes[1].astype(F32) * both[:, half:]
    out[...] = ((total + before[0]) * scale).astype(out.dtype)


def final_curvature(x_and_half, pieces, kinds, before, acts, probes, scale, dtype):
    _, half = pieces[0].shape[-2:]
    width, tokens = acts.shape
    block = 512
    return pl.pallas_call(
        functools.partial(final_body, kinds, scale),
        out_shape=jax.ShapeDtypeStruct((width, half), dtype),
        grid_spec=pltpu.PrefetchScalarGridSpec(
            num_scalar_prefetch=1,
            grid=(width // block,),
            in_specs=[ANY] * 5
            + [
                pl.BlockSpec((1, block, half), lambda d, at: (at[1], d, 0)),
                pl.BlockSpec((block, tokens), lambda d, at: (d, 0)),
                pl.BlockSpec((2, block, half), lambda d, at: (0, d, at[1])),
            ],
            out_specs=pl.BlockSpec((block, half), lambda d, at: (d, 0)),
            scratch_shapes=[pltpu.VMEM((HALF, tokens, 2 * half), BF16), pltpu.SemaphoreType.DMA((4, 2, 2))],
        ),
        cost_estimate=pl.CostEstimate(
            flops=4 * tokens * width * half, transcendentals=0, bytes_accessed=12 * width * half
        ),
        compiler_params=grant(16),
        name="final_curvature",
    )(x_and_half, *pieces, before, acts, probes)


def moved(axis, to):
    size = lax.axis_size(axis)
    pairs = [(i, to(i) % size) for i in range(size)]
    return lambda value: lax.ppermute(value, axis, pairs)


def program(activations, cotangent, gate_w, up_w, down_w, probes):
    s, width = activations.shape[1:]
    rows = lax.axis_size("row")
    z_step = 4
    partner = moved("row", lambda i: i ^ 1)
    across = moved("row", lambda i: i ^ 2)
    z_up, z_down = moved("row", lambda i: i + z_step), moved("row", lambda i: i - z_step)
    z_far = moved("row", lambda i: i + 2 * z_step)
    x_up, x_down = moved("col", lambda i: i + 1), moved("col", lambda i: i - 1)
    x_far = moved("col", lambda i: i + 2)
    other_group = moved("dp", lambda i: i + 1)

    col, group = lax.axis_index("col"), lax.axis_index("dp")
    x = jnp.stack([col, jnp.zeros_like(col)]).astype(jnp.int32)
    x_other = jnp.stack([col, 1 - group]).astype(jnp.int32)
    x_mine = jnp.stack([col, group]).astype(jnp.int32)
    weights = (gate_w, up_w, down_w, probes)

    mine = pack(activations, cotangent)
    beside = across(mine)
    below, above = z_up(mine), z_down(mine)
    first = [mine, beside, below, above]
    first += [partner(part) for part in first]
    below_beside, above_beside = z_up(beside), z_down(beside)
    opposite, opposite_beside = z_up(below), z_down(above_beside)
    second = [below_beside, above_beside, opposite, opposite_beside]
    second += [partner(part) for part in second]

    def ring_start(sources):
        acts, right, left, middle, own = partials(x, sources, *weights)
        return acts, x_up(right), x_down(left), middle, own

    def ring_sum(right, left, middle, own, kinds):
        far_right = x_up((middle[0] + right[0].astype(F32)).astype(BF16))
        far_left = x_down((middle[1] + left[0].astype(F32)).astype(BF16))
        return terms(own, right, left, far_right, far_left, kinds)

    def ring_gather(piece):
        from_left, from_right = x_up(piece), x_down(piece)
        far_left, far_right = x_up(from_left[0]), x_down(from_right[1])
        return piece, from_left, from_right, far_left, far_right

    acts_a, right_a, left_a, middle_a, own_a = ring_start(first)
    acts_b, right_b, left_b, middle_b, own_b = ring_start(second)
    acts_a, acts_b = flip(acts_a), flip(acts_b)
    (piece_a,) = ring_sum(right_a, left_a, middle_a, own_a, (3,))
    pieces_a = ring_gather(piece_a)
    hidden_b, weighted_b = ring_sum(right_b, left_b, middle_b, own_b, (1, 2))
    far_b = x_far(hidden_b)
    hiddens_b = (hidden_b, x_up(hidden_b), x_down(hidden_b), far_b, far_b)
    weighteds_b = ring_gather(weighted_b)

    def halves_summed(pieces):
        kept, sent = outputs_part(x, pieces, down_w)
        return (kept + partner(sent)).reshape(4, s, width)

    sum_a = halves_summed(pieces_a)
    from_above, from_below = z_down(sum_a[2].astype(BF16)), z_up(sum_a[3].astype(BF16))
    total = curvature(x, pieces_a, (1, 2), acts_a, probes)

    sum_b = halves_summed(hiddens_b)
    near = sum_a[0] + from_above.astype(F32) + from_below.astype(F32)
    from_far = z_far(sum_b[2:].astype(BF16))
    beside_above, beside_below = z_down(sum_b[0].astype(BF16)), z_up(sum_b[1].astype(BF16))
    near = near + from_far[0].astype(F32)
    other = sum_a[1] + beside_above.astype(F32) + beside_below.astype(F32) + from_far[1].astype(F32)
    outputs = near + across(other.astype(BF16)).astype(F32)

    scale = 1.0 / (probes.shape[0] * lax.axis_size("dp") * s * rows)
    sent = final_curvature(x_other, weighteds_b, (0, 1), total, acts_b, probes, scale, BF16)
    arrived = other_group(sent)
    kept = final_curvature(x_mine, weighteds_b, (0, 1), total, acts_b, probes, scale, F32)
    return outputs.astype(BF16)[None], kept + arrived.astype(F32)


def solution(mesh):
    in_specs = (
        P("dp", "row", "col"),
        P("dp", "row", "col"),
        P("col", "row"),
        P("col", "row"),
        P("row", "col"),
        P(None, "col", "row"),
    )
    out_specs = (P("dp", "row", "col"), P("col", ("row", "dp")))
    return jax.shard_map(program, mesh=mesh, in_specs=in_specs, out_specs=out_specs, check_vma=False)
```

```python
import functools

import jax
import jax.numpy as jnp
from jax import lax
from jax.experimental import pallas as pl
from jax.experimental.pallas import tpu as pltpu
from jax.sharding import PartitionSpec as P


F32, BF16 = jnp.float32, jnp.bfloat16
HBM = pl.BlockSpec(memory_space=pltpu.MemorySpace.HBM)
VMEM = pl.BlockSpec(memory_space=pltpu.MemorySpace.VMEM)
COLS, HALF = 4, 2


def grant(mebibytes):
    return pltpu.CompilerParams(vmem_limit_bytes=mebibytes << 20)


def in_hbm(value):
    return pltpu.with_memory_space_constraint(value, pltpu.MemorySpace.HBM)


def pack_body(acts, cots, out, sems):
    copies = [pltpu.make_async_copy(part.at[0], out.at[k], sems.at[k]) for k, part in enumerate((acts, cots))]
    for copy in copies:
        copy.start()
    for copy in copies:
        copy.wait()


def pack(acts, cots):
    return pl.pallas_call(
        pack_body,
        in_specs=[HBM, HBM],
        out_specs=VMEM,
        out_shape=jax.ShapeDtypeStruct((2, *acts.shape[1:]), acts.dtype),
        scratch_shapes=[pltpu.SemaphoreType.DMA((2,))],
        compiler_params=grant(4),
        name="pack",
    )(in_hbm(acts), in_hbm(cots))


def partials_body(count, groups, at, *refs):
    sources = refs[:count]
    gate_w, up_w, down_w, probes = refs[count : count + 4]
    acts, *outs = refs[count + 4 : count + 5 + 4 * len(groups)]
    cots, weights, down, total, sems = refs[count + 5 + 4 * len(groups) :]
    x = at[0]
    shard = sources[0].shape[1]
    quarter = shard * count // COLS

    loads = [
        pltpu.make_async_copy(src, into, sems.at[k])
        for k, (src, into) in enumerate(
            (
                (gate_w, weights.at[0]),
                (up_w, weights.at[1]),
                (probes.at[0], weights.at[2]),
                (probes.at[1], weights.at[3]),
                (down_w, down),
            )
        )
    ]
    for copy in loads:
        copy.start()
    for s, src in enumerate(sources):
        acts[s * shard : (s + 1) * shard] = src[0]
        cots[s * shard : (s + 1) * shard] = src[1]

    def rows(r):
        return pl.ds(pl.multiple_of(lax.rem(x + r, COLS) * quarter, 16), quarter)

    for g, group in enumerate(groups):
        right, left, middle, own = outs[4 * g : 4 * g + 4]
        half = right.shape[-1]
        lo, hi = slice(0, half), slice(half, 2 * half)
        for n, k in enumerate(group):
            loads[k].wait()
            part = total.at[k % 2]
            if k < 4:
                part[...] = jnp.dot(acts[...], weights[k], preferred_element_type=F32)
            else:
                part[...] = lax.dot_general(cots[...], down[...], (((1,), (1,)), ((), ())), preferred_element_type=F32)
            right[0, n] = part[rows(2), lo].astype(BF16)
            right[1, n] = part[rows(1), hi].astype(BF16)
            left[0, n] = part[rows(2), hi].astype(BF16)
            left[1, n] = part[rows(3), lo].astype(BF16)
            middle[0, n] = part[rows(1), lo]
            middle[1, n] = part[rows(3), hi]
            own[n] = part[rows(0), :]


def partials(x, sources, groups, gate_w, up_w, down_w, probes):
    shard, width = sources[0].shape[1:]
    hidden = gate_w.shape[1]
    tokens = shard * len(sources)
    quarter, half = tokens // COLS, hidden // HALF
    shapes = [((tokens, width), BF16)]
    for group in groups:
        message = (2, len(group), quarter, half)
        shapes += [(message, BF16), (message, BF16), (message, F32), ((len(group), quarter, hidden), F32)]
    return pl.pallas_call(
        functools.partial(partials_body, len(sources), groups),
        out_shape=[jax.ShapeDtypeStruct(*shape) for shape in shapes],
        grid_spec=pltpu.PrefetchScalarGridSpec(
            num_scalar_prefetch=1,
            grid=(),
            in_specs=[VMEM] * len(sources) + [HBM] * 4,
            out_specs=[VMEM] * len(shapes),
            scratch_shapes=[
                pltpu.VMEM((tokens, width), BF16),
                pltpu.VMEM((4, width, hidden), BF16),
                pltpu.VMEM((hidden, width), BF16),
                pltpu.VMEM((2, tokens, hidden), F32),
                pltpu.SemaphoreType.DMA((5,)),
            ],
        ),
        cost_estimate=pl.CostEstimate(
            flops=10 * tokens * width * hidden,
            transcendentals=0,
            bytes_accessed=10 * width * hidden + 22 * tokens * hidden,
        ),
        compiler_params=grant(24),
        name="partials",
    )(x, *sources, *map(in_hbm, (gate_w, up_w, down_w, probes)))


def over_rows(quarter, do):
    block = 16 * (2 - quarter // 16 % 2)

    def some_rows(n, carry):
        do(pl.ds(pl.multiple_of(n * block, block), block))
        return carry

    lax.fori_loop(0, quarter // block, some_rows, 0)


def total_of(own, near, far, h, i, rows):
    half = far.shape[-1]
    return own[i, rows, h * half : (h + 1) * half] + near[1, i, rows].astype(F32) + far[i, rows].astype(F32)


def hidden_and_slope(gate, up):
    sigma = 1.0 / (1.0 + jnp.exp(-gate))
    return gate * sigma * up, up * sigma * (1.0 - sigma) * (2.0 + gate * (1.0 - 2.0 * sigma))


def terms_body(own, right, left, far_right, far_left, out):
    def do(rows):
        for h, near, far in ((0, left, far_right), (1, right, far_left)):
            gate, up, first, second, error = (total_of(own, near, far, h, i, rows) for i in range(5))
            hidden, slope = hidden_and_slope(gate, up)
            bending = error * slope
            for k, value in enumerate((hidden, bending * first, bending * second)):
                out[h, k, rows] = value.astype(BF16)

    over_rows(own.shape[1], do)


def hidden_body(own, right, left, far_right, far_left, out, slopes):
    def do(rows):
        for h, near, far in ((0, left, far_right), (1, right, far_left)):
            hidden, slope = hidden_and_slope(*(total_of(own, near, far, h, i, rows) for i in range(2)))
            out[h, 0, rows] = hidden.astype(BF16)
            slopes[h, rows] = slope

    over_rows(own.shape[1], do)


def weighted_body(own, right, left, far_right, far_left, slopes, out):
    def do(rows):
        for h, near, far in ((0, left, far_right), (1, right, far_left)):
            first, second, error = (total_of(own, near, far, h, i, rows) for i in range(3))
            bending = error * slopes[h, rows]
            out[h, 0, rows] = (bending * first).astype(BF16)
            out[h, 1, rows] = (bending * second).astype(BF16)

    over_rows(own.shape[1], do)


def terms(body, own, *arrived, kinds, slopes=False):
    count, quarter, hidden = own.shape
    half = hidden // HALF
    shapes = [jax.ShapeDtypeStruct((HALF, kinds, quarter, half), BF16)]
    if slopes:
        shapes.append(jax.ShapeDtypeStruct((HALF, quarter, half), F32))
    return pl.pallas_call(
        body,
        in_specs=[VMEM] * (1 + len(arrived)),
        out_specs=[VMEM] * len(shapes),
        out_shape=shapes,
        cost_estimate=pl.CostEstimate(
            flops=20 * quarter * hidden, transcendentals=quarter * hidden, bytes_accessed=9 * count * quarter * hidden
        ),
        compiler_params=grant(12),
        name="terms",
    )(own, *arrived)


def flip_body(acts, out):
    out[...] = acts[...].T


def flip(acts):
    tokens, width = acts.shape
    block = 256
    return pl.pallas_call(
        flip_body,
        grid=(width // block,),
        in_specs=[pl.BlockSpec((tokens, block), lambda d: (0, d))],
        out_specs=pl.BlockSpec((block, tokens), lambda d: (d, 0)),
        out_shape=jax.ShapeDtypeStruct((width, tokens), acts.dtype),
        compiler_params=grant(12),
        name="flip",
    )(acts)


def gathered(x, pieces, kinds, store):
    mine, from_left, from_right, far_lo, far_hi = pieces
    quarter = mine.shape[-2]
    for r, parts in ((0, (mine, mine)), (3, (from_left,) * 2), (1, (from_right,) * 2), (2, (far_lo, far_hi))):
        rows = pl.ds(pl.multiple_of(lax.rem(x + r, COLS) * quarter, 16), quarter)
        for h, part in enumerate(parts):
            for place, kind in enumerate(kinds):
                store(h, place, rows, part[h, kind] if len(part.shape) == 4 else part[kind])


def outputs_body(kind, at, *refs):
    pieces, down, kept, sent, hidden = refs[:5], *refs[5:]
    half = pieces[0].shape[-1]

    @pl.when(pl.program_id(0) == 0)
    def _():
        def store(h, k, rows, value):
            hidden[rows, h * half : (h + 1) * half] = value

        gathered(at[0], pieces, (kind,), store)

    result = jnp.dot(hidden[...], down[...], preferred_element_type=F32)
    count = kept.shape[0]
    kept[...] = result[:count]
    sent[...] = result[count:]


def outputs_part(x, pieces, down_w, kind=0):
    quarter, half = pieces[0].shape[-2:]
    tokens, hidden, width = COLS * quarter, HALF * half, down_w.shape[1]
    block = 512
    side = jax.ShapeDtypeStruct((tokens // 2, width), F32)
    spec = pl.BlockSpec((tokens // 2, block), lambda d, at: (0, d))
    return pl.pallas_call(
        functools.partial(outputs_body, kind),
        out_shape=(side, side),
        grid_spec=pltpu.PrefetchScalarGridSpec(
            num_scalar_prefetch=1,
            grid=(width // block,),
            in_specs=[VMEM] * 5 + [pl.BlockSpec((hidden, block), lambda d, at: (0, d))],
            out_specs=(spec, spec),
            scratch_shapes=[pltpu.VMEM((tokens, hidden), BF16)],
        ),
        cost_estimate=pl.CostEstimate(
            flops=2 * tokens * width * hidden, transcendentals=0, bytes_accessed=2 * width * hidden + 4 * tokens * hidden
        ),
        compiler_params=grant(12),
        name="outputs_part",
    )(x, *pieces, down_w)


def curvature_body(kinds, at, *refs):
    pieces, acts, probes, out, weighted = refs[:5], *refs[5:]
    half = pieces[0].shape[-1]

    @pl.when(pl.program_id(0) == 0)
    def _():
        def store(h, k, rows, value):
            weighted[rows, (2 * h + k) * half : (2 * h + k + 1) * half] = value

        gathered(at[0], pieces, kinds, store)

    both = jnp.dot(acts[...], weighted[...], preferred_element_type=F32)
    for h in range(HALF):
        cols = slice(h * half, (h + 1) * half)
        first, second = (both[:, (2 * h + k) * half : (2 * h + k + 1) * half] for k in range(2))
        out[h] = probes[0, :, cols].astype(F32) * first + probes[1, :, cols].astype(F32) * second


def curvature(x, pieces, kinds, acts, probes):
    _, half = pieces[0].shape[-2:]
    width, tokens = acts.shape
    hidden, block = HALF * half, 256
    return pl.pallas_call(
        functools.partial(curvature_body, kinds),
        out_shape=jax.ShapeDtypeStruct((HALF, width, half), F32),
        grid_spec=pltpu.PrefetchScalarGridSpec(
            num_scalar_prefetch=1,
            grid=(width // block,),
            in_specs=[VMEM] * 5
            + [
                pl.BlockSpec((block, tokens), lambda d, at: (d, 0)),
                pl.BlockSpec((2, block, hidden), lambda d, at: (0, d, 0)),
            ],
            out_specs=pl.BlockSpec((HALF, block, half), lambda d, at: (0, d, 0)),
            scratch_shapes=[pltpu.VMEM((tokens, 2 * hidden), BF16)],
        ),
        cost_estimate=pl.CostEstimate(
            flops=4 * tokens * width * hidden, transcendentals=0, bytes_accessed=12 * width * hidden
        ),
        compiler_params=grant(16),
        name="curvature",
    )(x, *pieces, in_hbm(acts), in_hbm(probes))


def final_body(kinds, scale, at, *refs):
    pieces, before, acts, probes, out, weighted = refs[:5], *refs[5:]
    half = pieces[0].shape[-1]
    wanted = at[1]

    @pl.when(pl.program_id(0) == 0)
    def _():
        def store(h, k, rows, value):
            @pl.when(wanted == h)
            def _():
                weighted[rows, k * half : (k + 1) * half] = value

        gathered(at[0], pieces, kinds, store)

    both = jnp.dot(acts[...], weighted[...], preferred_element_type=F32)
    total = probes[0].astype(F32) * both[:, :half] + probes[1].astype(F32) * both[:, half:]
    out[...] = ((total + before[0]) * scale).astype(out.dtype)


def final_curvature(x_and_half, pieces, kinds, before, acts, probes, scale, dtype):
    _, half = pieces[0].shape[-2:]
    width, tokens = acts.shape
    block = 512
    return pl.pallas_call(
        functools.partial(final_body, kinds, scale),
        out_shape=jax.ShapeDtypeStruct((width, half), dtype),
        grid_spec=pltpu.PrefetchScalarGridSpec(
            num_scalar_prefetch=1,
            grid=(width // block,),
            in_specs=[VMEM] * 5
            + [
                pl.BlockSpec((1, block, half), lambda d, at: (at[1], d, 0)),
                pl.BlockSpec((block, tokens), lambda d, at: (d, 0)),
                pl.BlockSpec((2, block, half), lambda d, at: (0, d, at[1])),
            ],
            out_specs=pl.BlockSpec((block, half), lambda d, at: (d, 0)),
            scratch_shapes=[pltpu.VMEM((tokens, 2 * half), BF16)],
        ),
        cost_estimate=pl.CostEstimate(
            flops=4 * tokens * width * half, transcendentals=0, bytes_accessed=12 * width * half
        ),
        compiler_params=grant(16),
        name="final_curvature",
    )(x_and_half, *pieces, in_hbm(before), in_hbm(acts), in_hbm(probes))


def moved(axis, to):
    size = lax.axis_size(axis)
    pairs = [(i, to(i) % size) for i in range(size)]
    return lambda value: lax.ppermute(value, axis, pairs)


def program(activations, cotangent, gate_w, up_w, down_w, probes):
    s, width = activations.shape[1:]
    rows = lax.axis_size("row")
    z_step = 4
    partner = moved("row", lambda i: i ^ 1)
    across = moved("row", lambda i: i ^ 2)
    z_up, z_down = moved("row", lambda i: i + z_step), moved("row", lambda i: i - z_step)
    z_far = moved("row", lambda i: i + 2 * z_step)
    x_up, x_down = moved("col", lambda i: i + 1), moved("col", lambda i: i - 1)
    x_far = moved("col", lambda i: i + 2)
    other_group = moved("dp", lambda i: i + 1)

    col, group = lax.axis_index("col"), lax.axis_index("dp")
    x = jnp.stack([col, jnp.zeros_like(col)]).astype(jnp.int32)
    x_other = jnp.stack([col, 1 - group]).astype(jnp.int32)
    x_mine = jnp.stack([col, group]).astype(jnp.int32)
    weights = (gate_w, up_w, down_w, probes)

    mine = pack(activations, cotangent)
    beside = across(mine)
    below, above = z_up(mine), z_down(mine)
    first = [mine, beside, below, above]
    first += [partner(part) for part in first]
    below_beside, above_beside = z_up(beside), z_down(beside)
    opposite, opposite_beside = z_up(below), z_down(above_beside)
    second = [below_beside, above_beside, opposite, opposite_beside]
    second += [partner(part) for part in second]

    def hops(right, left):
        return x_up(right), x_down(left)

    def ring_sum(right, left, middle, own):
        right, left = hops(right, left)
        far_right = (middle[0] + right[0].astype(F32)).astype(BF16)
        far_left = (middle[1] + left[0].astype(F32)).astype(BF16)
        return own, right, left, *hops(far_right, far_left)

    def ring_gather(piece):
        from_left, from_right = x_up(piece), x_down(piece)
        far_left, far_right = x_up(from_left[0]), x_down(from_right[1])
        return piece, from_left, from_right, far_left, far_right

    acts_a, *group = partials(x, first, ((0, 1, 2, 3, 4),), *weights)
    arrived_a = ring_sum(*group)
    acts_b, *groups = partials(x, second, ((0, 1), (2, 3, 4)), *weights)
    acts_a, acts_b = flip(acts_a), flip(acts_b)
    arrived_h, arrived_w = ring_sum(*groups[:4]), ring_sum(*groups[4:])

    (piece_a,) = terms(terms_body, *arrived_a, kinds=3)
    pieces_a = ring_gather(piece_a)
    hidden_b, slopes_b = terms(hidden_body, *arrived_h, kinds=1, slopes=True)
    far_b = x_far(hidden_b)
    hiddens_b = (hidden_b, x_up(hidden_b), x_down(hidden_b), far_b, far_b)
    (weighted_b,) = terms(weighted_body, *arrived_w, slopes_b, kinds=2)
    weighteds_b = ring_gather(weighted_b)

    def halves_summed(pieces):
        kept, sent = outputs_part(x, pieces, down_w)
        return (kept + partner(sent)).reshape(4, s, width)

    sum_a = halves_summed(pieces_a)
    from_above, from_below = z_down(sum_a[2].astype(BF16)), z_up(sum_a[3].astype(BF16))
    total = curvature(x, pieces_a, (1, 2), acts_a, probes)

    sum_b = halves_summed(hiddens_b)
    near = sum_a[0] + from_above.astype(F32) + from_below.astype(F32)
    from_far = z_far(sum_b[2:].astype(BF16))
    beside_above, beside_below = z_down(sum_b[0].astype(BF16)), z_up(sum_b[1].astype(BF16))
    near = near + from_far[0].astype(F32)
    other = sum_a[1] + beside_above.astype(F32) + beside_below.astype(F32) + from_far[1].astype(F32)
    outputs = near + across(other.astype(BF16)).astype(F32)

    scale = 1.0 / (probes.shape[0] * lax.axis_size("dp") * s * rows)
    sent = final_curvature(x_other, weighteds_b, (0, 1), total, acts_b, probes, scale, BF16)
    arrived = other_group(sent)
    kept = final_curvature(x_mine, weighteds_b, (0, 1), total, acts_b, probes, scale, F32)
    return outputs.astype(BF16)[None], kept + arrived.astype(F32)


def solution(mesh):
    in_specs = (
        P("dp", "row", "col"),
        P("dp", "row", "col"),
        P("col", "row"),
        P("col", "row"),
        P("row", "col"),
        P(None, "col", "row"),
    )
    out_specs = (P("dp", "row", "col"), P("col", ("row", "dp")))
    return jax.shard_map(program, mesh=mesh, in_specs=in_specs, out_specs=out_specs, check_vma=False)
```

```python
import functools

import jax
import jax.numpy as jnp
from jax import lax
from jax.experimental import pallas as pl
from jax.experimental.pallas import tpu as pltpu
from jax.sharding import PartitionSpec as P


F32, BF16 = jnp.float32, jnp.bfloat16
HBM = pl.BlockSpec(memory_space=pltpu.MemorySpace.HBM)
VMEM = pl.BlockSpec(memory_space=pltpu.MemorySpace.VMEM)
COLS, HALF = 4, 2


def grant(mebibytes):
    return pltpu.CompilerParams(vmem_limit_bytes=mebibytes << 20)


def in_hbm(value):
    return pltpu.with_memory_space_constraint(value, pltpu.MemorySpace.HBM)


def pack_body(acts, cots, out, sems):
    copies = [pltpu.make_async_copy(part.at[0], out.at[k], sems.at[k]) for k, part in enumerate((acts, cots))]
    for copy in copies:
        copy.start()
    for copy in copies:
        copy.wait()


def pack(acts, cots):
    return pl.pallas_call(
        pack_body,
        in_specs=[HBM, HBM],
        out_specs=VMEM,
        out_shape=jax.ShapeDtypeStruct((2, *acts.shape[1:]), acts.dtype),
        scratch_shapes=[pltpu.SemaphoreType.DMA((2,))],
        compiler_params=grant(4),
        name="pack",
    )(in_hbm(acts), in_hbm(cots))


def partials_body(count, groups, at, *refs):
    sources = refs[:count]
    gate_w, up_w, down_w, probes = refs[count : count + 4]
    acts, *outs = refs[count + 4 : count + 5 + 4 * len(groups)]
    cots, weights, down, total, sems = refs[count + 5 + 4 * len(groups) :]
    x = at[0]
    shard = sources[0].shape[1]
    quarter = shard * count // COLS

    loads = [
        pltpu.make_async_copy(src, into, sems.at[k])
        for k, (src, into) in enumerate(
            (
                (gate_w, weights.at[0]),
                (up_w, weights.at[1]),
                (probes.at[0], weights.at[2]),
                (probes.at[1], weights.at[3]),
                (down_w, down),
            )
        )
    ]
    for copy in loads:
        copy.start()
    for s, src in enumerate(sources):
        acts[s * shard : (s + 1) * shard] = src[0]
        cots[s * shard : (s + 1) * shard] = src[1]

    def rows(r):
        return pl.ds(pl.multiple_of(lax.rem(x + r, COLS) * quarter, 16), quarter)

    for g, group in enumerate(groups):
        right, left, middle, own = outs[4 * g : 4 * g + 4]
        half = right.shape[-1]
        lo, hi = slice(0, half), slice(half, 2 * half)
        for n, k in enumerate(group):
            loads[k].wait()
            part = total.at[k % 2]
            if k < 4:
                part[...] = jnp.dot(acts[...], weights[k], preferred_element_type=F32)
            else:
                part[...] = lax.dot_general(cots[...], down[...], (((1,), (1,)), ((), ())), preferred_element_type=F32)
            right[0, n] = part[rows(2), lo].astype(BF16)
            right[1, n] = part[rows(1), hi].astype(BF16)
            left[0, n] = part[rows(2), hi].astype(BF16)
            left[1, n] = part[rows(3), lo].astype(BF16)
            middle[0, n] = part[rows(1), lo]
            middle[1, n] = part[rows(3), hi]
            own[n] = part[rows(0), :]


def partials(x, sources, groups, gate_w, up_w, down_w, probes):
    shard, width = sources[0].shape[1:]
    hidden = gate_w.shape[1]
    tokens = shard * len(sources)
    quarter, half = tokens // COLS, hidden // HALF
    shapes = [((tokens, width), BF16)]
    for group in groups:
        message = (2, len(group), quarter, half)
        shapes += [(message, BF16), (message, BF16), (message, F32), ((len(group), quarter, hidden), F32)]
    return pl.pallas_call(
        functools.partial(partials_body, len(sources), groups),
        out_shape=[jax.ShapeDtypeStruct(*shape) for shape in shapes],
        grid_spec=pltpu.PrefetchScalarGridSpec(
            num_scalar_prefetch=1,
            grid=(),
            in_specs=[VMEM] * len(sources) + [HBM] * 4,
            out_specs=[VMEM] * len(shapes),
            scratch_shapes=[
                pltpu.VMEM((tokens, width), BF16),
                pltpu.VMEM((4, width, hidden), BF16),
                pltpu.VMEM((hidden, width), BF16),
                pltpu.VMEM((2, tokens, hidden), F32),
                pltpu.SemaphoreType.DMA((5,)),
            ],
        ),
        cost_estimate=pl.CostEstimate(
            flops=10 * tokens * width * hidden,
            transcendentals=0,
            bytes_accessed=10 * width * hidden + 22 * tokens * hidden,
        ),
        compiler_params=grant(24),
        name="partials",
    )(x, *sources, *map(in_hbm, (gate_w, up_w, down_w, probes)))


def over_rows(quarter, do):
    block = 16 * (2 - quarter // 16 % 2)

    def some_rows(n, carry):
        do(pl.ds(pl.multiple_of(n * block, block), block))
        return carry

    lax.fori_loop(0, quarter // block, some_rows, 0)


def total_of(own, near, far, h, i, rows):
    half = far.shape[-1]
    return own[i, rows, h * half : (h + 1) * half] + near[1, i, rows].astype(F32) + far[i, rows].astype(F32)


def hidden_and_slope(gate, up):
    sigma = 1.0 / (1.0 + jnp.exp(-gate))
    return gate * sigma * up, up * sigma * (1.0 - sigma) * (2.0 + gate * (1.0 - 2.0 * sigma))


def terms_body(own, right, left, far_right, far_left, out):
    def do(rows):
        for h, near, far in ((0, left, far_right), (1, right, far_left)):
            gate, up, first, second, error = (total_of(own, near, far, h, i, rows) for i in range(5))
            hidden, slope = hidden_and_slope(gate, up)
            bending = error * slope
            for k, value in enumerate((hidden, bending * first, bending * second)):
                out[h, k, rows] = value.astype(BF16)

    over_rows(own.shape[1], do)


def hidden_body(own, right, left, far_right, far_left, out, slopes):
    def do(rows):
        for h, near, far in ((0, left, far_right), (1, right, far_left)):
            hidden, slope = hidden_and_slope(*(total_of(own, near, far, h, i, rows) for i in range(2)))
            out[h, 0, rows] = hidden.astype(BF16)
            slopes[h, rows] = slope

    over_rows(own.shape[1], do)


def weighted_body(own, right, left, far_right, far_left, slopes, out):
    def do(rows):
        for h, near, far in ((0, left, far_right), (1, right, far_left)):
            first, second, error = (total_of(own, near, far, h, i, rows) for i in range(3))
            bending = error * slopes[h, rows]
            out[h, 0, rows] = (bending * first).astype(BF16)
            out[h, 1, rows] = (bending * second).astype(BF16)

    over_rows(own.shape[1], do)


def terms(body, own, *arrived, kinds, slopes=False):
    count, quarter, hidden = own.shape
    half = hidden // HALF
    shapes = [jax.ShapeDtypeStruct((HALF, kinds, quarter, half), BF16)]
    if slopes:
        shapes.append(jax.ShapeDtypeStruct((HALF, quarter, half), F32))
    return pl.pallas_call(
        body,
        in_specs=[VMEM] * (1 + len(arrived)),
        out_specs=[VMEM] * len(shapes),
        out_shape=shapes,
        cost_estimate=pl.CostEstimate(
            flops=20 * quarter * hidden, transcendentals=quarter * hidden, bytes_accessed=9 * count * quarter * hidden
        ),
        compiler_params=grant(12),
        name="terms",
    )(own, *arrived)


def flip_body(acts, out):
    out[...] = acts[...].T


def flip(acts):
    tokens, width = acts.shape
    block = 256
    return pl.pallas_call(
        flip_body,
        grid=(width // block,),
        in_specs=[pl.BlockSpec((tokens, block), lambda d: (0, d))],
        out_specs=pl.BlockSpec((block, tokens), lambda d: (d, 0)),
        out_shape=jax.ShapeDtypeStruct((width, tokens), acts.dtype),
        compiler_params=grant(12),
        name="flip",
    )(acts)


def gathered(x, pieces, kinds, store):
    mine, from_left, from_right, far_lo, far_hi = pieces
    quarter = mine.shape[-2]
    for r, parts in ((0, (mine, mine)), (3, (from_left,) * 2), (1, (from_right,) * 2), (2, (far_lo, far_hi))):
        rows = pl.ds(pl.multiple_of(lax.rem(x + r, COLS) * quarter, 16), quarter)
        for h, part in enumerate(parts):
            for place, kind in enumerate(kinds):
                store(h, place, rows, part[h, kind] if len(part.shape) == 4 else part[kind])


def outputs_body(kind, at, *refs):
    pieces, down, kept, sent, hidden = refs[:5], *refs[5:]
    half = pieces[0].shape[-1]

    @pl.when(pl.program_id(0) == 0)
    def _():
        def store(h, k, rows, value):
            hidden[rows, h * half : (h + 1) * half] = value

        gathered(at[0], pieces, (kind,), store)

    result = jnp.dot(hidden[...], down[...], preferred_element_type=F32)
    count = kept.shape[0]
    kept[...] = result[:count]
    sent[...] = result[count:]


def outputs_part(x, pieces, down_w, kind=0):
    quarter, half = pieces[0].shape[-2:]
    tokens, hidden, width = COLS * quarter, HALF * half, down_w.shape[1]
    block = 512
    side = jax.ShapeDtypeStruct((tokens // 2, width), F32)
    spec = pl.BlockSpec((tokens // 2, block), lambda d, at: (0, d))
    return pl.pallas_call(
        functools.partial(outputs_body, kind),
        out_shape=(side, side),
        grid_spec=pltpu.PrefetchScalarGridSpec(
            num_scalar_prefetch=1,
            grid=(width // block,),
            in_specs=[VMEM] * 5 + [pl.BlockSpec((hidden, block), lambda d, at: (0, d))],
            out_specs=(spec, spec),
            scratch_shapes=[pltpu.VMEM((tokens, hidden), BF16)],
        ),
        cost_estimate=pl.CostEstimate(
            flops=2 * tokens * width * hidden, transcendentals=0, bytes_accessed=2 * width * hidden + 4 * tokens * hidden
        ),
        compiler_params=grant(12),
        name="outputs_part",
    )(x, *pieces, down_w)


def curvature_body(kinds, scale, started, at, *refs):
    pieces, rest = refs[:5], list(refs[5:])
    before = rest.pop(0) if started else None
    acts, probes, out, weighted = rest
    half = pieces[0].shape[-1]
    wanted = at[1]

    @pl.when(pl.program_id(0) == 0)
    def _():
        def store(h, k, rows, value):
            @pl.when(wanted == h)
            def _():
                weighted[rows, k * half : (k + 1) * half] = value

        gathered(at[0], pieces, kinds, store)

    both = jnp.dot(acts[...], weighted[...], preferred_element_type=F32)
    total = probes[0].astype(F32) * both[:, :half] + probes[1].astype(F32) * both[:, half:]
    if started:
        total = total + before[...]
    if scale is not None:
        total = total * scale
    out[...] = total.astype(out.dtype)


def curvature(x_and_half, pieces, kinds, before, acts, probes, scale=None, dtype=F32):
    _, half = pieces[0].shape[-2:]
    width, tokens = acts.shape
    block = 512
    started = before is not None
    spec = pl.BlockSpec((block, half), lambda d, at: (d, 0))
    return pl.pallas_call(
        functools.partial(curvature_body, kinds, scale, started),
        out_shape=jax.ShapeDtypeStruct((width, half), dtype),
        grid_spec=pltpu.PrefetchScalarGridSpec(
            num_scalar_prefetch=1,
            grid=(width // block,),
            in_specs=[VMEM] * 5
            + [spec] * started
            + [
                pl.BlockSpec((block, tokens), lambda d, at: (d, 0)),
                pl.BlockSpec((2, block, half), lambda d, at: (0, d, at[1])),
            ],
            out_specs=spec,
            scratch_shapes=[pltpu.VMEM((tokens, 2 * half), BF16)],
        ),
        cost_estimate=pl.CostEstimate(
            flops=4 * tokens * width * half, transcendentals=0, bytes_accessed=12 * width * half
        ),
        compiler_params=grant(16),
        name="curvature",
    )(x_and_half, *pieces, *([before] * started), in_hbm(acts), in_hbm(probes))


def moved(axis, to):
    size = lax.axis_size(axis)
    pairs = [(i, to(i) % size) for i in range(size)]
    return lambda value: lax.ppermute(value, axis, pairs)


def program(activations, cotangent, gate_w, up_w, down_w, probes):
    s, width = activations.shape[1:]
    rows = lax.axis_size("row")
    z_step = 4
    partner = moved("row", lambda i: i ^ 1)
    across = moved("row", lambda i: i ^ 2)
    z_up, z_down = moved("row", lambda i: i + z_step), moved("row", lambda i: i - z_step)
    z_far = moved("row", lambda i: i + 2 * z_step)
    x_up, x_down = moved("col", lambda i: i + 1), moved("col", lambda i: i - 1)
    x_far = moved("col", lambda i: i + 2)
    other_group = moved("dp", lambda i: i + 1)

    col, group = lax.axis_index("col"), lax.axis_index("dp")
    x = jnp.stack([col, jnp.zeros_like(col)]).astype(jnp.int32)
    x_other = jnp.stack([col, 1 - group]).astype(jnp.int32)
    x_mine = jnp.stack([col, group]).astype(jnp.int32)
    weights = (gate_w, up_w, down_w, probes)

    mine = pack(activations, cotangent)
    beside = across(mine)
    below, above = z_up(mine), z_down(mine)
    first = [mine, beside, below, above]
    first += [partner(part) for part in first]
    below_beside, above_beside = z_up(beside), z_down(beside)
    opposite, opposite_beside = z_up(below), z_down(above_beside)
    second = [below_beside, above_beside, opposite, opposite_beside]
    second += [partner(part) for part in second]

    def hops(right, left):
        return x_up(right), x_down(left)

    def ring_sum(right, left, middle, own):
        right, left = hops(right, left)
        far_right = (middle[0] + right[0].astype(F32)).astype(BF16)
        far_left = (middle[1] + left[0].astype(F32)).astype(BF16)
        return own, right, left, *hops(far_right, far_left)

    def ring_gather(piece):
        from_left, from_right = x_up(piece), x_down(piece)
        far_left, far_right = x_up(from_left[0]), x_down(from_right[1])
        return piece, from_left, from_right, far_left, far_right

    acts_a, *group = partials(x, first, ((0, 1, 2, 3, 4),), *weights)
    arrived_a = ring_sum(*group)
    acts_b, *groups = partials(x, second, ((0, 1), (2, 3, 4)), *weights)
    acts_a, acts_b = flip(acts_a), flip(acts_b)
    arrived_h, arrived_w = ring_sum(*groups[:4]), ring_sum(*groups[4:])

    (piece_a,) = terms(terms_body, *arrived_a, kinds=3)
    pieces_a = ring_gather(piece_a)
    hidden_b, slopes_b = terms(hidden_body, *arrived_h, kinds=1, slopes=True)
    far_b = x_far(hidden_b)
    hiddens_b = (hidden_b, x_up(hidden_b), x_down(hidden_b), far_b, far_b)
    (weighted_b,) = terms(weighted_body, *arrived_w, slopes_b, kinds=2)
    weighteds_b = ring_gather(weighted_b)

    def halves_summed(pieces):
        kept, sent = outputs_part(x, pieces, down_w)
        return (kept + partner(sent)).reshape(4, s, width)

    sum_b = halves_summed(hiddens_b)
    from_far = z_far(sum_b[2:].astype(BF16))
    beside_above, beside_below = z_down(sum_b[0].astype(BF16)), z_up(sum_b[1].astype(BF16))
    sum_a = halves_summed(pieces_a)
    from_above, from_below = z_down(sum_a[2].astype(BF16)), z_up(sum_a[3].astype(BF16))
    other = sum_a[1] + beside_above.astype(F32) + beside_below.astype(F32) + from_far[1].astype(F32)
    near = sum_a[0] + from_far[0].astype(F32)
    near = near + across(other.astype(BF16)).astype(F32)
    outputs = near + from_above.astype(F32) + from_below.astype(F32)

    scale = 1.0 / (probes.shape[0] * lax.axis_size("dp") * s * rows)
    sent = curvature(x_other, pieces_a, (1, 2), None, acts_a, probes)
    sent = curvature(x_other, weighteds_b, (0, 1), sent, acts_b, probes, scale, BF16)
    arrived = other_group(sent)
    kept = curvature(x_mine, pieces_a, (1, 2), None, acts_a, probes)
    kept = curvature(x_mine, weighteds_b, (0, 1), kept, acts_b, probes, scale, F32)
    return outputs.astype(BF16)[None], kept + arrived.astype(F32)


def solution(mesh):
    in_specs = (
        P("dp", "row", "col"),
        P("dp", "row", "col"),
        P("col", "row"),
        P("col", "row"),
        P("row", "col"),
        P(None, "col", "row"),
    )
    out_specs = (P("dp", "row", "col"), P("col", ("row", "dp")))
    return jax.shard_map(program, mesh=mesh, in_specs=in_specs, out_specs=out_specs, check_vma=False)
```

```python
import functools

import jax
import jax.numpy as jnp
from jax import lax
from jax.experimental import pallas as pl
from jax.experimental.pallas import tpu as pltpu
from jax.sharding import PartitionSpec as P


F32, BF16 = jnp.float32, jnp.bfloat16
HBM = pl.BlockSpec(memory_space=pltpu.MemorySpace.HBM)
VMEM = pl.BlockSpec(memory_space=pltpu.MemorySpace.VMEM)
SMEM = pl.BlockSpec(memory_space=pltpu.MemorySpace.SMEM)
COLS, HALF = 4, 2


def grant(mebibytes):
    return pltpu.CompilerParams(vmem_limit_bytes=mebibytes << 20)


def in_hbm(value):
    return pltpu.with_memory_space_constraint(value, pltpu.MemorySpace.HBM)


def pack_body(acts, cots, out, sems):
    copies = [pltpu.make_async_copy(part.at[0], out.at[k], sems.at[k]) for k, part in enumerate((acts, cots))]
    for copy in copies:
        copy.start()
    for copy in copies:
        copy.wait()


def pack(acts, cots):
    return pl.pallas_call(
        pack_body,
        in_specs=[HBM, HBM],
        out_specs=VMEM,
        out_shape=jax.ShapeDtypeStruct((2, *acts.shape[1:]), acts.dtype),
        scratch_shapes=[pltpu.SemaphoreType.DMA((2,))],
        compiler_params=grant(4),
        name="pack",
    )(in_hbm(acts), in_hbm(cots))


def partials_body(count, groups, at, *refs):
    sources = refs[:count]
    gate_w, up_w, down_w, probes = refs[count : count + 4]
    acts, *outs = refs[count + 4 : count + 5 + 4 * len(groups)]
    cots, weights, down, total, sems = refs[count + 5 + 4 * len(groups) :]
    x = at[0]
    shard = sources[0].shape[1]
    quarter = shard * count // COLS

    loads = [
        pltpu.make_async_copy(src, into, sems.at[k])
        for k, (src, into) in enumerate(
            (
                (gate_w, weights.at[0]),
                (up_w, weights.at[1]),
                (probes.at[0], weights.at[2]),
                (probes.at[1], weights.at[3]),
                (down_w, down),
            )
        )
    ]
    for copy in loads:
        copy.start()
    for s, src in enumerate(sources):
        acts[s * shard : (s + 1) * shard] = src[0]
        cots[s * shard : (s + 1) * shard] = src[1]

    def rows(r):
        return pl.ds(pl.multiple_of(lax.rem(x + r, COLS) * quarter, 16), quarter)

    for g, group in enumerate(groups):
        right, left, middle, own = outs[4 * g : 4 * g + 4]
        half = right.shape[-1]
        lo, hi = slice(0, half), slice(half, 2 * half)
        for n, k in enumerate(group):
            loads[k].wait()
            part = total.at[k % 2]
            if k < 4:
                part[...] = jnp.dot(acts[...], weights[k], preferred_element_type=F32)
            else:
                part[...] = lax.dot_general(cots[...], down[...], (((1,), (1,)), ((), ())), preferred_element_type=F32)
            right[0, n] = part[rows(2), lo].astype(BF16)
            right[1, n] = part[rows(1), hi].astype(BF16)
            left[0, n] = part[rows(2), hi].astype(BF16)
            left[1, n] = part[rows(3), lo].astype(BF16)
            middle[0, n] = part[rows(1), lo]
            middle[1, n] = part[rows(3), hi]
            own[n] = part[rows(0), :]


def partials(x, sources, groups, gate_w, up_w, down_w, probes):
    shard, width = sources[0].shape[1:]
    hidden = gate_w.shape[1]
    tokens = shard * len(sources)
    quarter, half = tokens // COLS, hidden // HALF
    shapes = [((tokens, width), BF16)]
    for group in groups:
        message = (2, len(group), quarter, half)
        shapes += [(message, BF16), (message, BF16), (message, F32), ((len(group), quarter, hidden), F32)]
    return pl.pallas_call(
        functools.partial(partials_body, len(sources), groups),
        out_shape=[jax.ShapeDtypeStruct(*shape) for shape in shapes],
        grid_spec=pltpu.PrefetchScalarGridSpec(
            num_scalar_prefetch=1,
            grid=(),
            in_specs=[VMEM] * len(sources) + [HBM] * 4,
            out_specs=[VMEM] * len(shapes),
            scratch_shapes=[
                pltpu.VMEM((tokens, width), BF16),
                pltpu.VMEM((4, width, hidden), BF16),
                pltpu.VMEM((hidden, width), BF16),
                pltpu.VMEM((2, tokens, hidden), F32),
                pltpu.SemaphoreType.DMA((5,)),
            ],
        ),
        cost_estimate=pl.CostEstimate(
            flops=10 * tokens * width * hidden,
            transcendentals=0,
            bytes_accessed=10 * width * hidden + 22 * tokens * hidden,
        ),
        compiler_params=grant(30),
        name="partials",
    )(x, *sources, *map(in_hbm, (gate_w, up_w, down_w, probes)))


def over_rows(quarter, do):
    block = 16 * (2 - quarter // 16 % 2)

    def some_rows(n, carry):
        do(pl.ds(pl.multiple_of(n * block, block), block))
        return carry

    lax.fori_loop(0, quarter // block, some_rows, 0)


def total_of(own, near, far, h, i, rows):
    half = far.shape[-1]
    return own[i, rows, h * half : (h + 1) * half] + near[1, i, rows].astype(F32) + far[i, rows].astype(F32)


def hidden_and_slope(gate, up):
    sigma = 1.0 / (1.0 + jnp.exp(-gate))
    return gate * sigma * up, up * sigma * (1.0 - sigma) * (2.0 + gate * (1.0 - 2.0 * sigma))


def terms_body(own, right, left, far_right, far_left, out):
    def do(rows):
        for h, near, far in ((0, left, far_right), (1, right, far_left)):
            gate, up, first, second, error = (total_of(own, near, far, h, i, rows) for i in range(5))
            hidden, slope = hidden_and_slope(gate, up)
            bending = error * slope
            for k, value in enumerate((hidden, bending * first, bending * second)):
                out[h, k, rows] = value.astype(BF16)

    over_rows(own.shape[1], do)


def hidden_body(own, right, left, far_right, far_left, out, slopes):
    def do(rows):
        for h, near, far in ((0, left, far_right), (1, right, far_left)):
            hidden, slope = hidden_and_slope(*(total_of(own, near, far, h, i, rows) for i in range(2)))
            out[h, 0, rows] = hidden.astype(BF16)
            slopes[h, rows] = slope

    over_rows(own.shape[1], do)


def weighted_body(at, own, right, left, far_right, far_left, slopes, other, mine):
    def do(rows):
        for h, near, far in ((0, left, far_right), (1, right, far_left)):
            first, second, error = (total_of(own, near, far, h, i, rows) for i in range(3))
            bending = error * slopes[h, rows]
            values = (bending * first).astype(BF16), (bending * second).astype(BF16)
            for kept, out in ((True, mine), (False, other)):

                @pl.when((at[1] == h) == kept)
                def _(out=out, values=values):
                    out[0, rows], out[1, rows] = values

    over_rows(own.shape[1], do)


def terms(body, own, *arrived, outs, scalars=()):
    count, quarter, hidden = own.shape
    half = hidden // HALF
    return pl.pallas_call(
        body,
        in_specs=[SMEM] * len(scalars) + [VMEM] * (1 + len(arrived)),
        out_specs=[VMEM] * len(outs),
        out_shape=[jax.ShapeDtypeStruct((*lead, quarter, half), dtype) for lead, dtype in outs],
        cost_estimate=pl.CostEstimate(
            flops=20 * quarter * hidden, transcendentals=quarter * hidden, bytes_accessed=9 * count * quarter * hidden
        ),
        compiler_params=grant(14),
        name="terms",
    )(*scalars, own, *arrived)


def flip_body(acts, out):
    out[...] = acts[...].T


def flip(acts):
    tokens, width = acts.shape
    block = 256
    return pl.pallas_call(
        flip_body,
        grid=(width // block,),
        in_specs=[pl.BlockSpec((tokens, block), lambda d: (0, d))],
        out_specs=pl.BlockSpec((block, tokens), lambda d: (d, 0)),
        out_shape=jax.ShapeDtypeStruct((width, tokens), acts.dtype),
        compiler_params=grant(12),
        name="flip",
    )(acts)


def gathered(x, pieces, kinds, store):
    mine, from_left, from_right, far_lo, far_hi = pieces
    quarter = mine.shape[-2]
    halves = range(HALF) if len(mine.shape) == 4 else (None,)
    for r, parts in ((0, (mine, mine)), (3, (from_left,) * 2), (1, (from_right,) * 2), (2, (far_lo, far_hi))):
        rows = pl.ds(pl.multiple_of(lax.rem(x + r, COLS) * quarter, 16), quarter)
        for h in halves:
            part = parts[h or 0]
            for place, kind in enumerate(kinds):
                store(h, place, rows, part[h, kind] if len(part.shape) == 4 else part[kind])


def outputs_body(kind, at, *refs):
    pieces, down, kept, sent, hidden = refs[:5], *refs[5:]
    half = pieces[0].shape[-1]

    @pl.when(pl.program_id(0) == 0)
    def _():
        def store(h, k, rows, value):
            hidden[rows, h * half : (h + 1) * half] = value

        gathered(at[0], pieces, (kind,), store)

    result = jnp.dot(hidden[...], down[...], preferred_element_type=F32)
    count = kept.shape[0]
    kept[...] = result[:count]
    sent[...] = result[count:]


def outputs_part(x, pieces, down_w, kind=0):
    quarter, half = pieces[0].shape[-2:]
    tokens, hidden, width = COLS * quarter, HALF * half, down_w.shape[1]
    block = 512
    side = jax.ShapeDtypeStruct((tokens // 2, width), F32)
    spec = pl.BlockSpec((tokens // 2, block), lambda d, at: (0, d))
    return pl.pallas_call(
        functools.partial(outputs_body, kind),
        out_shape=(side, side),
        grid_spec=pltpu.PrefetchScalarGridSpec(
            num_scalar_prefetch=1,
            grid=(width // block,),
            in_specs=[VMEM] * 5 + [pl.BlockSpec((hidden, block), lambda d, at: (0, d))],
            out_specs=(spec, spec),
            scratch_shapes=[pltpu.VMEM((tokens, hidden), BF16)],
        ),
        cost_estimate=pl.CostEstimate(
            flops=2 * tokens * width * hidden, transcendentals=0, bytes_accessed=2 * width * hidden + 4 * tokens * hidden
        ),
        compiler_params=grant(12),
        name="outputs_part",
    )(x, *pieces, down_w)


def curvature_body(kinds, scale, started, at, *refs):
    pieces, rest = refs[:5], list(refs[5:])
    before = rest.pop(0) if started else None
    acts, probes, out, weighted = rest
    half = pieces[0].shape[-1]
    wanted = at[1]

    @pl.when(pl.program_id(0) == 0)
    def _():
        def store(h, k, rows, value):
            @pl.when(True if h is None else wanted == h)
            def _():
                weighted[rows, k * half : (k + 1) * half] = value

        gathered(at[0], pieces, kinds, store)

    both = jnp.dot(acts[...], weighted[...], preferred_element_type=F32)
    total = probes[0].astype(F32) * both[:, :half] + probes[1].astype(F32) * both[:, half:]
    if started:
        total = total + before[...]
    if scale is not None:
        total = total * scale
    out[...] = total.astype(out.dtype)


def curvature(x_and_half, pieces, kinds, before, acts, probes, scale=None, dtype=F32):
    _, half = pieces[0].shape[-2:]
    width, tokens = acts.shape
    block = 512
    started = before is not None
    spec = pl.BlockSpec((block, half), lambda d, at: (d, 0))
    return pl.pallas_call(
        functools.partial(curvature_body, kinds, scale, started),
        out_shape=jax.ShapeDtypeStruct((width, half), dtype),
        grid_spec=pltpu.PrefetchScalarGridSpec(
            num_scalar_prefetch=1,
            grid=(width // block,),
            in_specs=[VMEM] * 5
            + [spec] * started
            + [
                pl.BlockSpec((block, tokens), lambda d, at: (d, 0)),
                pl.BlockSpec((2, block, half), lambda d, at: (0, d, at[1])),
            ],
            out_specs=spec,
            scratch_shapes=[pltpu.VMEM((tokens, 2 * half), BF16)],
        ),
        cost_estimate=pl.CostEstimate(
            flops=4 * tokens * width * half, transcendentals=0, bytes_accessed=12 * width * half
        ),
        compiler_params=grant(16),
        name="curvature",
    )(x_and_half, *pieces, *([before] * started), in_hbm(acts), in_hbm(probes))


def moved(axis, to):
    size = lax.axis_size(axis)
    pairs = [(i, to(i) % size) for i in range(size)]
    return lambda value: lax.ppermute(value, axis, pairs)


def program(activations, cotangent, gate_w, up_w, down_w, probes):
    s, width = activations.shape[1:]
    rows = lax.axis_size("row")
    z_step = 4
    partner = moved("row", lambda i: i ^ 1)
    across = moved("row", lambda i: i ^ 2)
    z_up, z_down = moved("row", lambda i: i + z_step), moved("row", lambda i: i - z_step)
    z_far = moved("row", lambda i: i + 2 * z_step)
    x_up, x_down = moved("col", lambda i: i + 1), moved("col", lambda i: i - 1)
    x_far = moved("col", lambda i: i + 2)
    other_group = moved("dp", lambda i: i + 1)

    col, group = lax.axis_index("col"), lax.axis_index("dp")
    x = jnp.stack([col, jnp.zeros_like(col)]).astype(jnp.int32)
    x_other = jnp.stack([col, 1 - group]).astype(jnp.int32)
    x_mine = jnp.stack([col, group]).astype(jnp.int32)
    weights = (gate_w, up_w, down_w, probes)

    mine = pack(activations, cotangent)
    below, above = z_up(mine), z_down(mine)
    beside = across(mine)
    first = [mine, below, above]
    first += [partner(part) for part in first]
    below_beside, above_beside = z_up(beside), z_down(beside)
    opposite, opposite_beside = z_up(below), z_down(above_beside)
    second = [beside, below_beside, above_beside, opposite, opposite_beside]
    second += [partner(part) for part in second]

    def hops(right, left):
        return x_up(right), x_down(left)

    def ring_sum(right, left, middle, own):
        right, left = hops(right, left)
        far_right = (middle[0] + right[0].astype(F32)).astype(BF16)
        far_left = (middle[1] + left[0].astype(F32)).astype(BF16)
        return own, right, left, *hops(far_right, far_left)

    def ring_gather(piece):
        from_left, from_right = x_up(piece), x_down(piece)
        far_left, far_right = x_up(from_left[0]), x_down(from_right[1])
        return piece, from_left, from_right, far_left, far_right

    acts_a, *group = partials(x, first, ((0, 1, 2, 3, 4),), *weights)
    arrived_a = ring_sum(*group)
    acts_b, *groups = partials(x, second, ((0, 1), (2, 3, 4)), *weights)
    acts_a, acts_b = flip(acts_a), flip(acts_b)
    arrived_h, arrived_w = ring_sum(*groups[:4]), ring_sum(*groups[4:])

    (piece_a,) = terms(terms_body, *arrived_a, outs=(((HALF, 3), BF16),))
    pieces_a = ring_gather(piece_a)
    hidden_b, slopes_b = terms(hidden_body, *arrived_h, outs=(((HALF, 1), BF16), ((HALF,), F32)))
    other_b, mine_b = terms(weighted_body, *arrived_w, slopes_b, outs=(((2,), BF16), ((2,), BF16)), scalars=(x_mine,))

    def all_gather(piece):
        far = x_far(piece)
        return piece, x_up(piece), x_down(piece), far, far

    hiddens_b, others_b, mines_b = all_gather(hidden_b), all_gather(other_b), all_gather(mine_b)

    def halves_summed(pieces):
        kept, sent = outputs_part(x, pieces, down_w)
        return (kept + partner(sent)).reshape(-1, s, width)

    sum_b = halves_summed(hiddens_b)
    from_far = z_far(sum_b[3:].astype(BF16))
    beside_above, beside_below = z_down(sum_b[1].astype(BF16)), z_up(sum_b[2].astype(BF16))
    sum_a = halves_summed(pieces_a)
    from_above, from_below = z_down(sum_a[1].astype(BF16)), z_up(sum_a[2].astype(BF16))
    near = sum_a[0] + from_above.astype(F32) + from_below.astype(F32)
    other = sum_b[0] + beside_above.astype(F32) + beside_below.astype(F32) + from_far[1].astype(F32)
    near = near + from_far[0].astype(F32)
    outputs = near + across(other.astype(BF16)).astype(F32)

    scale = 1.0 / (probes.shape[0] * lax.axis_size("dp") * s * rows)
    sent = curvature(x_other, pieces_a, (1, 2), None, acts_a, probes)
    sent = curvature(x_other, others_b, (0, 1), sent, acts_b, probes, scale, BF16)
    arrived = other_group(sent)
    kept = curvature(x_mine, pieces_a, (1, 2), None, acts_a, probes)
    kept = curvature(x_mine, mines_b, (0, 1), kept, acts_b, probes, scale, F32)
    return outputs.astype(BF16)[None], kept + arrived.astype(F32)


def solution(mesh):
    in_specs = (
        P("dp", "row", "col"),
        P("dp", "row", "col"),
        P("col", "row"),
        P("col", "row"),
        P("row", "col"),
        P(None, "col", "row"),
    )
    out_specs = (P("dp", "row", "col"), P("col", ("row", "dp")))
    return jax.shard_map(program, mesh=mesh, in_specs=in_specs, out_specs=out_specs, check_vma=False)
```
